256 devices in a mesh: ctx: 32 (over y, z), tp: 8 (over x, core).
Axes of the slice: x: 4, y: 4, z: 8, core: 2. Of those that a mesh axis runs over, the one named last changes fastest.
Arguments:
- queries: bfloat16 [8192, 8192], P('ctx', 'tp'), may hold values from -24 to 24
- keys: bfloat16 [8192, 1024], P('ctx', 'tp'), may hold values from -24 to 24
- values: bfloat16 [8192, 1024], P('ctx', 'tp'), may hold values from -6 to 6
- vertical: int32 [64, 8], P('tp'), may hold values from 0 to 127
- slash: int32 [64, 8], P('tp'), may hold values from 1 to 63
- block_position: int32 [128], replicated, may hold values from 0 to 127, as said below
- ssm_input: bfloat16 [8192, 16384], P('ctx', 'tp'), may hold values from -6 to 6
- gate: bfloat16 [8192, 16384], P('ctx', 'tp'), may hold values from -20 to 20
- state_in: bfloat16 [8192, 16], P('ctx'), may hold values from -6 to 6
- state_out: bfloat16 [8192, 16], P('ctx'), may hold values from -6 to 6
- step_size: float32 [8192, 256], P('ctx', 'tp'), may hold values from 0 to 10, as said below
- decay_log: float32 [256], P('tp'), may hold values from -3.2 to -2.5
- skip_gain: float32 [256], P('tp'), may hold values from 0.5 to 2
- norm_gain: float32 [16384], P('tp'), may hold values from 0.1 to 1.9
Outputs:
- attention_out: bfloat16 [8192, 8192], P('ctx', 'tp')
- recurrent_mixer_result: bfloat16 [8192, 16384], P('ctx', 'tp')
The draws below stay inside these ranges and needn't reach their ends.
Inputs may be any that keep to these rules, and one draw needn't show every extreme that they name: `vertical`: block indices of the sequence; a head may name a block twice. `block_position`: a permutation of the sequence's blocks; the m-th block stored on each index of ctx lies in the m-th group of as many consecutive blocks as ctx has devices. `step_size`: positive.
All inputs are finite; a program needn't handle non-finite values.
Results may differ from the reference program's by a relative error of at most 0.0054.
Values may be sent and summed in bfloat16 or wider, within the bound.
A program may use at most 128 MiB of HBM per device.

```python
import math
import jax
import jax.numpy as jnp
from jax import lax

HEADS = 64
KV_HEADS = 8
HEAD_DIM = 128
RECURRENT_LANES = 256
SSM_HEAD_DIM = 64
D_STATE = 16
BLOCK = 64
NV = 8
NS = 8
TOK_DEV = 256
PROMPT_WORD_COUNT = 8192
NB = 128
QW = 8192
KW = 1024
INNER = 16384


def draw_keys(key, part):
    drawn = jax.random.normal(jax.random.fold_in(key, 21), (PROMPT_WORD_COUNT, KV_HEADS * HEAD_DIM), jnp.float32)
    return jnp.clip(1.4 * drawn, -8.0, 8.0).astype(jnp.bfloat16)


def draw_queries(key, part):
    drawn = jax.random.normal(jax.random.fold_in(key, 22), (PROMPT_WORD_COUNT, HEADS * HEAD_DIM), jnp.float32)
    return jnp.clip(1.4 * drawn, -8.0, 8.0).astype(jnp.bfloat16)


def draw_block_position(key, part):
    per_device = TOK_DEV // BLOCK
    groups = NB // per_device
    subkeys = jax.random.split(jax.random.fold_in(key, 31), per_device)
    orders = jax.vmap(lambda subkey: jax.random.permutation(subkey, groups))(subkeys).astype(jnp.int32)
    placed = orders.T + (jnp.arange(per_device, dtype=jnp.int32) * groups)[None, :]
    return placed.reshape(NB).astype(jnp.int32)


def draw_gate(key, part):
    drawn = jax.random.normal(jax.random.fold_in(key, 41), (PROMPT_WORD_COUNT, INNER), jnp.float32)
    ramp = 3.0 ** (jnp.arange(INNER, dtype=jnp.float32) / (INNER - 1))
    jitter = jnp.exp(jax.random.uniform(jax.random.fold_in(key, 42), (INNER,), jnp.float32, -0.5, 0.5))
    return jnp.clip(drawn * ramp * jitter, -12.0, 12.0).astype(jnp.bfloat16)


def draw_step_size(key, part):
    coin = jax.random.uniform(jax.random.fold_in(key, 51), (RECURRENT_LANES,), jnp.float32)
    fast = coin < 0.5
    fast_base = jax.random.uniform(jax.random.fold_in(key, 52), (RECURRENT_LANES,), jnp.float32, 0.33, 0.55)
    slow_base = jax.random.uniform(jax.random.fold_in(key, 53), (RECURRENT_LANES,), jnp.float32, 0.15, 0.4) / (PROMPT_WORD_COUNT * 0.06)
    base = jnp.where(fast, fast_base, slow_base)
    rough = jax.random.uniform(jax.random.fold_in(key, 54), (PROMPT_WORD_COUNT, RECURRENT_LANES), jnp.float32, 0.5, 1.5)
    device_factor = jnp.exp(jax.random.uniform(jax.random.fold_in(key, 55), (PROMPT_WORD_COUNT // TOK_DEV, 1), jnp.float32, -0.7, 0.7))
    device_factor = jnp.repeat(device_factor, TOK_DEV, axis=0)
    uniform_stride_gap = base[None, :] * rough * device_factor
    cluster_opening_slot = jax.random.randint(jax.random.fold_in(key, 56), (3,), 0, PROMPT_WORD_COUNT)
    cluster_member_boolean = jnp.any(jnp.arange(PROMPT_WORD_COUNT, dtype=jnp.int32)[:, None] == cluster_opening_slot[None, :], axis=1)
    cluster_extent = jax.random.uniform(jax.random.fold_in(key, 57), (PROMPT_WORD_COUNT, RECURRENT_LANES), jnp.float32, 4.0, 10.0)
    return jnp.where(cluster_member_boolean[:, None], cluster_extent, uniform_stride_gap)


def place_ends(drawn, rng, least, high):
    longest = drawn.shape.index(max(drawn.shape))
    spots = []
    for shift in (0, 1):
        where = [jax.random.randint(jax.random.fold_in(rng, axis), (), 0, length) for axis, length in enumerate(drawn.shape)]
        where[longest] = (where[longest] + shift) % drawn.shape[longest]
        spots.append(tuple(where))
    return drawn.at[spots[0]].set(least).at[spots[1]].set(high)


def steps_of(stream_key, dims, pieces, least, high):
    loudness, own = 1.0, jax.random.fold_in(stream_key, 6)
    for dim, parts in pieces:
        steps = jnp.exp(jax.random.uniform(jax.random.fold_in(own, dim), (parts,), jnp.float32, least / len(pieces), high / len(pieces)))
        loudness = loudness * jnp.repeat(steps, dims[dim] // parts).reshape([-1 if axis == dim else 1 for axis in range(len(dims))])
    return loudness


def normal_values(key, dims, spread, most, cuts=(), kind=jnp.bfloat16):
    values = jax.random.normal(key, dims, jnp.float32) * spread
    if len(cuts) > 0:
        values = steps_of(key, dims, cuts, -0.22, 0.18) * values
    return jnp.clip(values, min=-most, max=most).astype(kind)


def setup_inputs(seed: int = 0) -> dict:
    streams_of = jax.random.split(jax.random.key(seed), 15)
    return {
        "queries": draw_queries(jax.random.fold_in(streams_of[14], 71), 0),
        "keys": draw_keys(jax.random.fold_in(streams_of[14], 71), 0),
        "values": normal_values(streams_of[2], (PROMPT_WORD_COUNT, KW), 1.0, 6.0, ((0, 32), (1, 8))),
        "vertical": place_ends(jax.random.randint(streams_of[3], (HEADS, NV), 0, NB), jax.random.fold_in(streams_of[3], 1), 0, NB - 1).astype(jnp.int32),
        "slash": place_ends(jax.random.randint(streams_of[4], (HEADS, NS), 1, NB // 2), jax.random.fold_in(streams_of[4], 1), 1, (NB // 2) - 1).astype(jnp.int32),
        "block_position": draw_block_position(jax.random.fold_in(streams_of[14], 71), 0),
        "ssm_input": normal_values(streams_of[6], (PROMPT_WORD_COUNT, INNER), 1.0, 6.0, ((0, 32), (1, 8))),
        "gate": draw_gate(jax.random.fold_in(streams_of[14], 71), 0),
        "state_in": normal_values(streams_of[8], (PROMPT_WORD_COUNT, D_STATE), 1.0, 6.0, ((0, 32),)),
        "state_out": normal_values(streams_of[9], (PROMPT_WORD_COUNT, D_STATE), 1.0, 6.0, ((0, 32),)),
        "step_size": draw_step_size(jax.random.fold_in(streams_of[14], 71), 0),
        "decay_log": jnp.clip(-3.2 + 0.70000005 * jax.random.uniform(streams_of[11], (RECURRENT_LANES,), jnp.float32) ** steps_of(streams_of[11], (RECURRENT_LANES,), ((0, 8),), -0.2, 0.2), -3.2, -2.5),
        "skip_gain": jnp.clip(0.5 + 1.5 * jax.random.uniform(streams_of[12], (RECURRENT_LANES,), jnp.float32) ** steps_of(streams_of[12], (RECURRENT_LANES,), ((0, 8),), -0.2, 0.2), 0.5, 2.0),
        "norm_gain": jnp.clip(1.0 + 0.18 * jax.random.normal(streams_of[13], (INNER,), jnp.float32), 0.1, 1.9),
    }


def block_allowed(block_pos, vertical_head, slash_head):
    in_vertical = jnp.any(block_pos[:, None] == vertical_head[None, :], axis=1)
    offset = block_pos[:, None] - block_pos[None, :]
    on_slash = jnp.any(offset[:, :, None] == slash_head[None, None, :], axis=2)
    return in_vertical[None, :] | on_slash | (offset == 0)

def reference(queries, keys, values, vertical, slash, block_position, ssm_input, gate, state_in, state_out, step_size, decay_log, skip_gain, norm_gain):
    offsets = jnp.arange(BLOCK, dtype=jnp.int32)
    tok_pos = (block_position.astype(jnp.int32)[:, None] * BLOCK + offsets[None, :]).reshape(PROMPT_WORD_COUNT)
    causal = tok_pos[None, :] <= tok_pos[:, None]
    group_size = HEADS // KV_HEADS
    score_scale = 1.0 / math.sqrt(HEAD_DIM)

    def one_head(head):
        q_head = lax.dynamic_slice_in_dim(queries, head * HEAD_DIM, HEAD_DIM, 1)
        kv_index = head // group_size
        k_head = lax.dynamic_slice_in_dim(keys, kv_index * HEAD_DIM, HEAD_DIM, 1)
        v_head = lax.dynamic_slice_in_dim(values, kv_index * HEAD_DIM, HEAD_DIM, 1)
        table = block_allowed(block_position, vertical[head], slash[head])
        allowed = jnp.repeat(jnp.repeat(table, BLOCK, axis=0), BLOCK, axis=1) & causal
        scores = jnp.dot(q_head, k_head.T, preferred_element_type=jnp.float32) * score_scale
        masked = jnp.where(allowed, scores, -1e+30)
        top_score = lax.optimization_barrier(jnp.max(masked, axis=1, keepdims=True))
        expo = jnp.where(allowed, jnp.exp(masked - top_score), 0.0)
        denominator = lax.optimization_barrier(jnp.sum(expo, axis=1, keepdims=True))
        output = jnp.dot(expo.astype(jnp.bfloat16), v_head, preferred_element_type=jnp.float32) / denominator
        return output.astype(jnp.bfloat16)
    head_outputs = lax.map(one_head, jnp.arange(HEADS, dtype=jnp.int32))
    attention_out = jnp.transpose(head_outputs, (1, 0, 2)).reshape(PROMPT_WORD_COUNT, QW)
    inputs = ssm_input.astype(jnp.float32).reshape(PROMPT_WORD_COUNT, RECURRENT_LANES, SSM_HEAD_DIM)
    decay_rate = jnp.exp(decay_log)

    def advance(state, sliced):
        x_now, b_now, c_now, dt_now = sliced
        retained = jnp.exp(-decay_rate * dt_now)
        state = retained[:, None, None] * state + (dt_now[:, None] * x_now)[:, :, None] * b_now[None, None, :]
        output = lax.optimization_barrier(jnp.sum(state * c_now[None, None, :], axis=2)) + skip_gain[:, None] * x_now
        return (state, output)
    initial = jnp.zeros((RECURRENT_LANES, SSM_HEAD_DIM, D_STATE), jnp.float32)
    _, mixed = lax.scan(advance, initial, (inputs, state_in.astype(jnp.float32), state_out.astype(jnp.float32), step_size))
    mixed = mixed.reshape(PROMPT_WORD_COUNT, INNER)
    gate_full = gate.astype(jnp.float32)
    gated = mixed * gate_full * jax.nn.sigmoid(gate_full)
    mean_square = lax.optimization_barrier(jnp.mean(gated * gated, axis=1, keepdims=True))
    recurrent_mixer_result = (gated * lax.rsqrt(mean_square + 1e-05) * norm_gain[None, :]).astype(jnp.bfloat16)
    return (attention_out, recurrent_mixer_result)
```

```python
import math

import jax
import jax.numpy as jnp
from jax import lax
from jax.experimental import pallas as pl
from jax.experimental.pallas import tpu as pltpu
from jax.sharding import PartitionSpec as P

HEAD_DIM = 128
SSM_HEAD_DIM = 64
D_STATE = 16
BLOCK = 64
INNER = 16384
NEG_FILL = -1e30


def shifted(array, axis, by):
    size = lax.axis_size(axis)
    pairs = [(i, i + by) for i in range(size) if 0 <= i + by < size]
    return lax.ppermute(array, axis, pairs)


def key_block_table(vertical, slash, block_position, blocks_here):
    my_index = lax.axis_index("ctx")
    total_blocks = block_position.shape[0]
    query_seq = lax.dynamic_slice_in_dim(block_position, my_index * blocks_here, blocks_here)
    storage_of = jnp.zeros((total_blocks,), jnp.int32).at[block_position].set(
        jnp.arange(total_blocks, dtype=jnp.int32)
    )
    heads = vertical.shape[0]
    br = query_seq[None, :, None]
    cand_v = jnp.broadcast_to(vertical[:, None, :], (heads, blocks_here, vertical.shape[1]))
    cand_s = br - slash[:, None, :]
    cand = jnp.concatenate([cand_v, cand_s], axis=-1)
    ok = jnp.concatenate([cand_v < br, cand_s >= 0], axis=-1)
    count = cand.shape[-1]
    earlier = jnp.arange(count)[None, :] < jnp.arange(count)[:, None]
    dup = jnp.any(
        (cand[..., :, None] == cand[..., None, :]) & ok[..., None, :] & earlier[None, None], axis=-1
    )
    ok = ok & ~dup
    diag = jnp.broadcast_to(query_seq[None, :, None], (heads, blocks_here, 1))
    cand = jnp.concatenate([diag, cand, jnp.zeros_like(diag)], axis=-1)
    ok = jnp.concatenate([jnp.ones_like(diag, bool), ok, jnp.zeros_like(diag, bool)], axis=-1)
    index = storage_of[jnp.clip(cand, 0, total_blocks - 1)]
    slots = cand.shape[-1]
    valid_cols = jnp.repeat(ok.astype(jnp.float32), BLOCK, axis=-1).reshape(heads * blocks_here, 1, slots * BLOCK)
    return index.reshape(-1).astype(jnp.int32), valid_cols, slots


def sparse_attention_kernel(slots, blocks_here, q_ref, kv_ref, idx_ref, valid_ref, o_ref, kbuf, vbuf):
    score_scale = 1.0 / math.sqrt(HEAD_DIM)
    width = slots * BLOCK
    units = valid_ref.shape[0]

    def unit(i, carry):
        head = i // blocks_here
        qblock = i % blocks_here
        for j in range(slots):
            src = pl.multiple_of(idx_ref[i * slots + j] * BLOCK, BLOCK)
            kbuf[pl.ds(j * BLOCK, BLOCK), :] = kv_ref[0, pl.ds(src, BLOCK), :]
            vbuf[pl.ds(j * BLOCK, BLOCK), :] = kv_ref[1, pl.ds(src, BLOCK), :]
        rows = pl.ds(pl.multiple_of(qblock * BLOCK, BLOCK), BLOCK)
        cols = pl.ds(pl.multiple_of(head * HEAD_DIM, HEAD_DIM), HEAD_DIM)
        q = q_ref[rows, cols]
        scores = lax.dot_general(
            q, kbuf[...], (((1,), (1,)), ((), ())), preferred_element_type=jnp.float32
        ) * score_scale
        r = lax.broadcasted_iota(jnp.int32, (BLOCK, width), 0)
        c = lax.broadcasted_iota(jnp.int32, (BLOCK, width), 1)
        allowed = ((c >= BLOCK) | (c <= r)) & (valid_ref[i] > 0.5)
        masked = jnp.where(allowed, scores, NEG_FILL)
        top = jnp.max(masked, axis=1, keepdims=True)
        expo = jnp.where(allowed, jnp.exp(masked - top), 0.0)
        denom = jnp.sum(expo, axis=1, keepdims=True)
        out = jnp.dot(expo.astype(jnp.bfloat16), vbuf[...], preferred_element_type=jnp.float32)
        o_ref[rows, cols] = (out / denom).astype(o_ref.dtype)
        return carry

    lax.fori_loop(0, units, unit, 0)


def attend_sparse(queries, keys, values, vertical, slash, block_position):
    row_count = queries.shape[0]
    blocks_here = row_count // BLOCK
    kv_all = lax.all_gather(jnp.stack((keys, values)), "ctx", axis=1, tiled=True)
    index, valid_cols, slots = key_block_table(vertical, slash, block_position, blocks_here)
    units = valid_cols.shape[0]
    flops = units * 4 * BLOCK * slots * BLOCK * HEAD_DIM
    return pl.pallas_call(
        lambda *refs: sparse_attention_kernel(slots, blocks_here, *refs),
        out_shape=jax.ShapeDtypeStruct(queries.shape, queries.dtype),
        in_specs=[
            pl.BlockSpec(memory_space=pltpu.VMEM),
            pl.BlockSpec(memory_space=pltpu.VMEM),
            pl.BlockSpec(memory_space=pltpu.SMEM),
            pl.BlockSpec(memory_space=pltpu.VMEM),
        ],
        out_specs=pl.BlockSpec(memory_space=pltpu.VMEM),
        scratch_shapes=[
            pltpu.VMEM((slots * BLOCK, HEAD_DIM), jnp.bfloat16),
            pltpu.VMEM((slots * BLOCK, HEAD_DIM), jnp.bfloat16),
        ],
        cost_estimate=pl.CostEstimate(
            flops=flops,
            transcendentals=units * BLOCK * slots * BLOCK,
            bytes_accessed=2 * queries.size * 2 + kv_all.size * 2,
        ),
    )(queries, kv_all, index, valid_cols)


def mamba_mix(ssm_input, gate, state_in, state_out, step_size, decay_log, skip_gain, norm_gain):
    careful = lax.Precision.HIGH
    row_count = ssm_input.shape[0]
    head_count = step_size.shape[1]
    inner_width = ssm_input.shape[1]
    inputs = ssm_input.astype(jnp.float32).reshape(row_count, head_count, SSM_HEAD_DIM)
    in_map = state_in.astype(jnp.float32)
    out_map = state_out.astype(jnp.float32)
    log_steps = -jnp.exp(decay_log)[None, :] * step_size
    cumulative = jnp.cumsum(log_steps, axis=0)
    grouped_per_head = cumulative.T
    lower = jnp.arange(row_count)[:, None] >= jnp.arange(row_count)[None, :]
    decay = jnp.where(
        lower[None],
        jnp.exp(jnp.minimum(grouped_per_head[:, :, None] - grouped_per_head[:, None, :], 0.0)),
        0.0,
    )
    inner = jnp.dot(state_out, state_in.T, preferred_element_type=jnp.float32)
    weighted = inputs * step_size[:, :, None]
    within = jnp.einsum("hts,shp->thp", decay * inner[None], weighted, precision=careful)
    tail = jnp.exp(cumulative[-1][None, :] - cumulative)
    local_state = jnp.einsum(
        "sn,shp->nhp", in_map, weighted * tail[:, :, None], precision=careful
    ).reshape(D_STATE, inner_width)
    carry_decay = jnp.repeat(jnp.exp(cumulative[-1]), SSM_HEAD_DIM)[None, :]

    packed = shifted(jnp.concatenate([carry_decay, local_state], axis=0), "ctx", 1)
    size = lax.axis_size("ctx")
    step = 1
    while step < size:
        got = shifted(packed, "ctx", step)
        factor = packed[0:1]
        packed = jnp.concatenate([factor * got[0:1], factor * got[1:] + packed[1:]], axis=0)
        step *= 2
    incoming = packed[1:]

    from_past = jnp.dot(
        out_map, incoming, precision=careful, preferred_element_type=jnp.float32
    ).reshape(row_count, head_count, SSM_HEAD_DIM)
    from_past = from_past * jnp.exp(cumulative)[:, :, None]
    mixed = (within + from_past + skip_gain[None, :, None] * inputs).reshape(row_count, inner_width)
    gate_full = gate.astype(jnp.float32)
    gated = mixed * gate_full * jax.nn.sigmoid(gate_full)
    squares = lax.psum(jnp.sum(gated * gated, axis=1), "tp")
    scaled = gated * lax.rsqrt(squares / INNER + 1e-05)[:, None] * norm_gain[None, :]
    return scaled.astype(jnp.bfloat16)


def local(
    queries,
    keys,
    values,
    vertical,
    slash,
    block_position,
    ssm_input,
    gate,
    state_in,
    state_out,
    step_size,
    decay_log,
    skip_gain,
    norm_gain,
):
    attention_out = attend_sparse(queries, keys, values, vertical, slash, block_position)
    recurrent_mixer_result = mamba_mix(
        ssm_input, gate, state_in, state_out, step_size, decay_log, skip_gain, norm_gain
    )
    return (attention_out, recurrent_mixer_result)


def solution(mesh):
    return jax.shard_map(
        local,
        mesh=mesh,
        in_specs=(
            P("ctx", "tp"),
            P("ctx", "tp"),
            P("ctx", "tp"),
            P("tp", None),
            P("tp", None),
            P(),
            P("ctx", "tp"),
            P("ctx", "tp"),
            P("ctx", None),
            P("ctx", None),
            P("ctx", "tp"),
            P("tp"),
            P("tp"),
            P("tp"),
        ),
        out_specs=(P("ctx", "tp"), P("ctx", "tp")),
        check_vma=False,
    )
```

```python
import math

import jax
import jax.numpy as jnp
from jax import lax
from jax.experimental import pallas as pl
from jax.experimental.pallas import tpu as pltpu
from jax.sharding import PartitionSpec as P

HEAD_DIM = 128
SSM_HEAD_DIM = 64
D_STATE = 16
BLOCK = 64
INNER = 16384
NEG_FILL = -1e30


def shifted(array, axis, by):
    size = lax.axis_size(axis)
    pairs = [(i, i + by) for i in range(size) if 0 <= i + by < size]
    return lax.ppermute(array, axis, pairs)


def key_block_table(vertical, slash, block_position, blocks_here):
    my_index = lax.axis_index("ctx")
    total_blocks = block_position.shape[0]
    query_seq = lax.dynamic_slice_in_dim(block_position, my_index * blocks_here, blocks_here)
    storage_of = jnp.zeros((total_blocks,), jnp.int32).at[block_position].set(
        jnp.arange(total_blocks, dtype=jnp.int32)
    )
    heads = vertical.shape[0]
    br = query_seq[None, :, None]
    cand_v = jnp.broadcast_to(vertical[:, None, :], (heads, blocks_here, vertical.shape[1]))
    cand_s = br - slash[:, None, :]
    cand = jnp.concatenate([cand_v, cand_s], axis=-1)
    ok = jnp.concatenate([cand_v < br, cand_s >= 0], axis=-1)
    count = cand.shape[-1]
    earlier = jnp.arange(count)[None, :] < jnp.arange(count)[:, None]
    dup = jnp.any(
        (cand[..., :, None] == cand[..., None, :]) & ok[..., None, :] & earlier[None, None], axis=-1
    )
    ok = ok & ~dup
    diag = jnp.broadcast_to(query_seq[None, :, None], (heads, blocks_here, 1))
    cand = jnp.concatenate([diag, cand, jnp.zeros_like(diag)], axis=-1)
    ok = jnp.concatenate([jnp.ones_like(diag, bool), ok, jnp.zeros_like(diag, bool)], axis=-1)
    index = storage_of[jnp.clip(cand, 0, total_blocks - 1)]
    slots = cand.shape[-1]
    col_bias = jnp.where(ok, 0.0, NEG_FILL).astype(jnp.float32)
    col_bias = jnp.repeat(col_bias, BLOCK, axis=-1).reshape(heads * blocks_here, 1, slots * BLOCK)
    return index.reshape(-1).astype(jnp.int32), col_bias, slots


def sparse_attention_kernel(slots, blocks_here, q_ref, kv_ref, idx_ref, bias_ref, causal_ref, o_ref, kbuf, vbuf):
    score_scale = 1.0 / math.sqrt(HEAD_DIM)
    units = bias_ref.shape[0]

    def unit(i, carry):
        head = i // blocks_here
        qblock = i % blocks_here
        for j in range(slots):
            src = pl.multiple_of(idx_ref[i * slots + j] * BLOCK, BLOCK)
            kbuf[pl.ds(j * BLOCK, BLOCK), :] = kv_ref[0, pl.ds(src, BLOCK), :]
            vbuf[pl.ds(j * BLOCK, BLOCK), :] = kv_ref[1, pl.ds(src, BLOCK), :]
        rows = pl.ds(pl.multiple_of(qblock * BLOCK, BLOCK), BLOCK)
        cols = pl.ds(pl.multiple_of(head * HEAD_DIM, HEAD_DIM), HEAD_DIM)
        q = q_ref[rows, cols]
        scores = lax.dot_general(
            q, kbuf[...], (((1,), (1,)), ((), ())), preferred_element_type=jnp.float32
        ) * score_scale
        masked = scores + causal_ref[...] + bias_ref[i]
        top = jnp.max(masked, axis=1, keepdims=True)
        expo = jnp.exp(masked - top)
        denom = jnp.sum(expo, axis=1, keepdims=True)
        out = jnp.dot(expo.astype(jnp.bfloat16), vbuf[...], preferred_element_type=jnp.float32)
        o_ref[rows, cols] = (out / denom).astype(o_ref.dtype)
        return carry

    lax.fori_loop(0, units, unit, 0, unroll=4)


def attend_sparse(queries, keys, values, vertical, slash, block_position):
    row_count = queries.shape[0]
    blocks_here = row_count // BLOCK
    kv_all = lax.all_gather(jnp.stack((keys, values)), "ctx", axis=1, tiled=True)
    index, col_bias, slots = key_block_table(vertical, slash, block_position, blocks_here)
    units = col_bias.shape[0]
    r = lax.broadcasted_iota(jnp.int32, (BLOCK, slots * BLOCK), 0)
    c = lax.broadcasted_iota(jnp.int32, (BLOCK, slots * BLOCK), 1)
    causal_bias = jnp.where((c < BLOCK) & (c > r), NEG_FILL, 0.0).astype(jnp.float32)
    flops = units * 4 * BLOCK * slots * BLOCK * HEAD_DIM
    return pl.pallas_call(
        lambda *refs: sparse_attention_kernel(slots, blocks_here, *refs),
        out_shape=jax.ShapeDtypeStruct(queries.shape, queries.dtype),
        in_specs=[
            pl.BlockSpec(memory_space=pltpu.VMEM),
            pl.BlockSpec(memory_space=pltpu.VMEM),
            pl.BlockSpec(memory_space=pltpu.SMEM),
            pl.BlockSpec(memory_space=pltpu.VMEM),
            pl.BlockSpec(memory_space=pltpu.VMEM),
        ],
        out_specs=pl.BlockSpec(memory_space=pltpu.VMEM),
        scratch_shapes=[
            pltpu.VMEM((slots * BLOCK, HEAD_DIM), jnp.bfloat16),
            pltpu.VMEM((slots * BLOCK, HEAD_DIM), jnp.bfloat16),
        ],
        cost_estimate=pl.CostEstimate(
            flops=flops,
            transcendentals=units * BLOCK * slots * BLOCK,
            bytes_accessed=2 * queries.size * 2 + kv_all.size * 2,
        ),
    )(queries, kv_all, index, col_bias, causal_bias)


def mamba_mix(ssm_input, gate, state_in, state_out, step_size, decay_log, skip_gain, norm_gain):
    careful = lax.Precision.HIGH
    row_count = ssm_input.shape[0]
    head_count = step_size.shape[1]
    inner_width = ssm_input.shape[1]
    inputs = ssm_input.astype(jnp.float32).reshape(row_count, head_count, SSM_HEAD_DIM)
    in_map = state_in.astype(jnp.float32)
    out_map = state_out.astype(jnp.float32)
    log_steps = -jnp.exp(decay_log)[None, :] * step_size
    cumulative = jnp.cumsum(log_steps, axis=0)
    grouped_per_head = cumulative.T
    lower = jnp.arange(row_count)[:, None] >= jnp.arange(row_count)[None, :]
    decay = jnp.where(
        lower[None],
        jnp.exp(jnp.minimum(grouped_per_head[:, :, None] - grouped_per_head[:, None, :], 0.0)),
        0.0,
    )
    inner = jnp.dot(state_out, state_in.T, preferred_element_type=jnp.float32)
    weighted = inputs * step_size[:, :, None]
    within = jnp.einsum("hts,shp->thp", decay * inner[None], weighted, precision=careful)
    tail = jnp.exp(cumulative[-1][None, :] - cumulative)
    local_state = jnp.einsum(
        "sn,shp->nhp", in_map, weighted * tail[:, :, None], precision=careful
    ).reshape(D_STATE, inner_width)
    carry_decay = jnp.repeat(jnp.exp(cumulative[-1]), SSM_HEAD_DIM)[None, :]

    packed = shifted(jnp.concatenate([carry_decay, local_state], axis=0), "ctx", 1)
    size = lax.axis_size("ctx")
    step = 1
    while step < size:
        got = shifted(packed, "ctx", step)
        factor = packed[0:1]
        packed = jnp.concatenate([factor * got[0:1], factor * got[1:] + packed[1:]], axis=0)
        step *= 2
    incoming = packed[1:]

    from_past = jnp.dot(
        out_map, incoming, precision=careful, preferred_element_type=jnp.float32
    ).reshape(row_count, head_count, SSM_HEAD_DIM)
    from_past = from_past * jnp.exp(cumulative)[:, :, None]
    mixed = (within + from_past + skip_gain[None, :, None] * inputs).reshape(row_count, inner_width)
    gate_full = gate.astype(jnp.float32)
    gated = mixed * gate_full * jax.nn.sigmoid(gate_full)
    squares = lax.psum(jnp.sum(gated * gated, axis=1), "tp")
    scaled = gated * lax.rsqrt(squares / INNER + 1e-05)[:, None] * norm_gain[None, :]
    return scaled.astype(jnp.bfloat16)


def local(
    queries,
    keys,
    values,
    vertical,
    slash,
    block_position,
    ssm_input,
    gate,
    state_in,
    state_out,
    step_size,
    decay_log,
    skip_gain,
    norm_gain,
):
    attention_out = attend_sparse(queries, keys, values, vertical, slash, block_position)
    recurrent_mixer_result = mamba_mix(
        ssm_input, gate, state_in, state_out, step_size, decay_log, skip_gain, norm_gain
    )
    return (attention_out, recurrent_mixer_result)


def solution(mesh):
    return jax.shard_map(
        local,
        mesh=mesh,
        in_specs=(
            P("ctx", "tp"),
            P("ctx", "tp"),
            P("ctx", "tp"),
            P("tp", None),
            P("tp", None),
            P(),
            P("ctx", "tp"),
            P("ctx", "tp"),
            P("ctx", None),
            P("ctx", None),
            P("ctx", "tp"),
            P("tp"),
            P("tp"),
            P("tp"),
        ),
        out_specs=(P("ctx", "tp"), P("ctx", "tp")),
        check_vma=False,
    )
```

```python
import math

import jax
import jax.numpy as jnp
from jax import lax
from jax.experimental import pallas as pl
from jax.experimental.pallas import tpu as pltpu
from jax.sharding import PartitionSpec as P

HEAD_DIM = 128
SSM_HEAD_DIM = 64
D_STATE = 16
BLOCK = 64
INNER = 16384
NEG_FILL = -1e30


def shifted(array, axis, by):
    size = lax.axis_size(axis)
    pairs = [(i, i + by) for i in range(size) if 0 <= i + by < size]
    return lax.ppermute(array, axis, pairs)


def key_block_table(vertical, slash, block_position, blocks_here):
    my_index = lax.axis_index("ctx")
    total_blocks = block_position.shape[0]
    query_seq = lax.dynamic_slice_in_dim(block_position, my_index * blocks_here, blocks_here)
    heads = vertical.shape[0]
    br = query_seq[None, :, None]
    cand_v = jnp.broadcast_to(vertical[:, None, :], (heads, blocks_here, vertical.shape[1]))
    cand_s = br - slash[:, None, :]
    cand = jnp.concatenate([cand_v, cand_s], axis=-1)
    ok = jnp.concatenate([cand_v < br, cand_s >= 0], axis=-1)
    count = cand.shape[-1]
    earlier = jnp.arange(count)[None, :] < jnp.arange(count)[:, None]
    dup = jnp.any(
        (cand[..., :, None] == cand[..., None, :]) & ok[..., None, :] & earlier[None, None], axis=-1
    )
    ok = ok & ~dup
    diag = jnp.broadcast_to(query_seq[None, :, None], (heads, blocks_here, 1))
    cand = jnp.concatenate([diag, cand, jnp.zeros_like(diag)], axis=-1)
    ok = jnp.concatenate([jnp.ones_like(diag, bool), ok, jnp.zeros_like(diag, bool)], axis=-1)
    match = block_position[None, None, None, :] == cand[..., None]
    index = jnp.sum(jnp.where(match, jnp.arange(total_blocks, dtype=jnp.int32), 0), axis=-1)
    slots = cand.shape[-1]
    col_bias = jnp.where(ok, 0.0, NEG_FILL).astype(jnp.float32)
    col_bias = jnp.repeat(col_bias, BLOCK, axis=-1).reshape(heads * blocks_here, 1, slots * BLOCK)
    return index.reshape(-1).astype(jnp.int32), col_bias, slots


def sparse_attention_kernel(slots, blocks_here, q_ref, kv_ref, idx_ref, bias_ref, causal_ref, o_ref, kbuf, vbuf):
    score_scale = 1.0 / math.sqrt(HEAD_DIM)
    units = bias_ref.shape[0]

    def unit(i, carry):
        head = i // blocks_here
        qblock = i % blocks_here
        for j in range(slots):
            src = pl.multiple_of(idx_ref[i * slots + j] * BLOCK, BLOCK)
            kbuf[pl.ds(j * BLOCK, BLOCK), :] = kv_ref[0, pl.ds(src, BLOCK), :]
            vbuf[pl.ds(j * BLOCK, BLOCK), :] = kv_ref[1, pl.ds(src, BLOCK), :]
        rows = pl.ds(pl.multiple_of(qblock * BLOCK, BLOCK), BLOCK)
        cols = pl.ds(pl.multiple_of(head * HEAD_DIM, HEAD_DIM), HEAD_DIM)
        q = q_ref[rows, cols]
        scores = lax.dot_general(
            q, kbuf[...], (((1,), (1,)), ((), ())), preferred_element_type=jnp.float32
        ) * score_scale
        masked = scores + causal_ref[...] + bias_ref[i]
        top = jnp.max(masked, axis=1, keepdims=True)
        expo = jnp.exp(masked - top)
        denom = jnp.sum(expo, axis=1, keepdims=True)
        out = jnp.dot(expo.astype(jnp.bfloat16), vbuf[...], preferred_element_type=jnp.float32)
        o_ref[rows, cols] = (out / denom).astype(o_ref.dtype)
        return carry

    lax.fori_loop(0, units, unit, 0, unroll=4)


def attend_sparse(queries, keys, values, vertical, slash, block_position):
    row_count = queries.shape[0]
    blocks_here = row_count // BLOCK
    kv_all = lax.all_gather(jnp.stack((keys, values)), "ctx", axis=1, tiled=True)
    index, col_bias, slots = key_block_table(vertical, slash, block_position, blocks_here)
    units = col_bias.shape[0]
    r = lax.broadcasted_iota(jnp.int32, (BLOCK, slots * BLOCK), 0)
    c = lax.broadcasted_iota(jnp.int32, (BLOCK, slots * BLOCK), 1)
    causal_bias = jnp.where((c < BLOCK) & (c > r), NEG_FILL, 0.0).astype(jnp.float32)
    flops = units * 4 * BLOCK * slots * BLOCK * HEAD_DIM
    return pl.pallas_call(
        lambda *refs: sparse_attention_kernel(slots, blocks_here, *refs),
        out_shape=jax.ShapeDtypeStruct(queries.shape, queries.dtype),
        in_specs=[
            pl.BlockSpec(memory_space=pltpu.VMEM),
            pl.BlockSpec(memory_space=pltpu.VMEM),
            pl.BlockSpec(memory_space=pltpu.SMEM),
            pl.BlockSpec(memory_space=pltpu.VMEM),
            pl.BlockSpec(memory_space=pltpu.VMEM),
        ],
        out_specs=pl.BlockSpec(memory_space=pltpu.VMEM),
        scratch_shapes=[
            pltpu.VMEM((slots * BLOCK, HEAD_DIM), jnp.bfloat16),
            pltpu.VMEM((slots * BLOCK, HEAD_DIM), jnp.bfloat16),
        ],
        cost_estimate=pl.CostEstimate(
            flops=flops,
            transcendentals=units * BLOCK * slots * BLOCK,
            bytes_accessed=2 * queries.size * 2 + kv_all.size * 2,
        ),
    )(queries, kv_all, index, col_bias, causal_bias)


def mamba_mix(ssm_input, gate, state_in, state_out, step_size, decay_log, skip_gain, norm_gain):
    careful = lax.Precision.HIGH
    row_count = ssm_input.shape[0]
    head_count = step_size.shape[1]
    inner_width = ssm_input.shape[1]
    inputs = ssm_input.astype(jnp.float32).reshape(row_count, head_count, SSM_HEAD_DIM)
    in_map = state_in.astype(jnp.float32)
    out_map = state_out.astype(jnp.float32)
    log_steps = -jnp.exp(decay_log)[None, :] * step_size
    cumulative = jnp.cumsum(log_steps, axis=0)
    grouped_per_head = cumulative.T
    lower = jnp.arange(row_count)[:, None] >= jnp.arange(row_count)[None, :]
    decay = jnp.where(
        lower[None],
        jnp.exp(jnp.minimum(grouped_per_head[:, :, None] - grouped_per_head[:, None, :], 0.0)),
        0.0,
    )
    inner = jnp.dot(state_out, state_in.T, preferred_element_type=jnp.float32)
    weighted = inputs * step_size[:, :, None]
    within = jnp.einsum("hts,shp->thp", decay * inner[None], weighted, precision=careful)
    tail = jnp.exp(cumulative[-1][None, :] - cumulative)
    local_state = jnp.einsum(
        "sn,shp->nhp", in_map, weighted * tail[:, :, None], precision=careful
    ).reshape(D_STATE, inner_width)
    carry_decay = jnp.repeat(jnp.exp(cumulative[-1]), SSM_HEAD_DIM)[None, :]

    packed = shifted(jnp.concatenate([carry_decay, local_state], axis=0), "ctx", 1)
    size = lax.axis_size("ctx")
    step = 1
    while step < size:
        got = shifted(packed, "ctx", step)
        factor = packed[0:1]
        packed = jnp.concatenate([factor * got[0:1], factor * got[1:] + packed[1:]], axis=0)
        step *= 2
    incoming = packed[1:]

    from_past = jnp.dot(
        out_map, incoming, precision=careful, preferred_element_type=jnp.float32
    ).reshape(row_count, head_count, SSM_HEAD_DIM)
    from_past = from_past * jnp.exp(cumulative)[:, :, None]
    mixed = (within + from_past + skip_gain[None, :, None] * inputs).reshape(row_count, inner_width)
    gate_full = gate.astype(jnp.float32)
    gated = mixed * gate_full * jax.nn.sigmoid(gate_full)
    squares = lax.psum(jnp.sum(gated * gated, axis=1), "tp")
    scaled = gated * lax.rsqrt(squares / INNER + 1e-05)[:, None] * norm_gain[None, :]
    return scaled.astype(jnp.bfloat16)


def local(
    queries,
    keys,
    values,
    vertical,
    slash,
    block_position,
    ssm_input,
    gate,
    state_in,
    state_out,
    step_size,
    decay_log,
    skip_gain,
    norm_gain,
):
    attention_out = attend_sparse(queries, keys, values, vertical, slash, block_position)
    recurrent_mixer_result = mamba_mix(
        ssm_input, gate, state_in, state_out, step_size, decay_log, skip_gain, norm_gain
    )
    return (attention_out, recurrent_mixer_result)


def solution(mesh):
    return jax.shard_map(
        local,
        mesh=mesh,
        in_specs=(
            P("ctx", "tp"),
            P("ctx", "tp"),
            P("ctx", "tp"),
            P("tp", None),
            P("tp", None),
            P(),
            P("ctx", "tp"),
            P("ctx", "tp"),
            P("ctx", None),
            P("ctx", None),
            P("ctx", "tp"),
            P("tp"),
            P("tp"),
            P("tp"),
        ),
        out_specs=(P("ctx", "tp"), P("ctx", "tp")),
        check_vma=False,
    )
```

```python
import math

import jax
import jax.numpy as jnp
from jax import lax
from jax.experimental import pallas as pl
from jax.experimental.pallas import tpu as pltpu
from jax.sharding import PartitionSpec as P

HEAD_DIM = 128
SSM_HEAD_DIM = 64
D_STATE = 16
BLOCK = 64
INNER = 16384
NEG_FILL = -1e30


def shifted(array, axis, by):
    size = lax.axis_size(axis)
    pairs = [(i, i + by) for i in range(size) if 0 <= i + by < size]
    return lax.ppermute(array, axis, pairs)


def key_block_table(vertical, slash, block_position, blocks_here):
    my_index = lax.axis_index("ctx")
    total_blocks = block_position.shape[0]
    query_seq = lax.dynamic_slice_in_dim(block_position, my_index * blocks_here, blocks_here)
    heads = vertical.shape[0]
    br = query_seq[None, :, None]
    cand_v = jnp.broadcast_to(vertical[:, None, :], (heads, blocks_here, vertical.shape[1]))
    cand_s = br - slash[:, None, :]
    cand = jnp.concatenate([cand_v, cand_s], axis=-1)
    ok = jnp.concatenate([cand_v < br, cand_s >= 0], axis=-1)
    count = cand.shape[-1]
    earlier = jnp.arange(count)[None, :] < jnp.arange(count)[:, None]
    dup = jnp.any(
        (cand[..., :, None] == cand[..., None, :]) & ok[..., None, :] & earlier[None, None], axis=-1
    )
    ok = ok & ~dup
    diag = jnp.broadcast_to(query_seq[None, :, None], (heads, blocks_here, 1))
    cand = jnp.concatenate([diag, cand, jnp.zeros_like(diag)], axis=-1)
    ok = jnp.concatenate([jnp.ones_like(diag, bool), ok, jnp.zeros_like(diag, bool)], axis=-1)
    match = block_position[None, None, None, :] == cand[..., None]
    index = jnp.sum(jnp.where(match, jnp.arange(total_blocks, dtype=jnp.int32), 0), axis=-1)
    slots = cand.shape[-1]
    col_bias = jnp.where(ok, 0.0, NEG_FILL).astype(jnp.float32)
    col_bias = jnp.repeat(col_bias, BLOCK, axis=-1).reshape(heads * blocks_here, 1, slots * BLOCK)
    return index.reshape(-1).astype(jnp.int32), col_bias, slots


def sparse_attention_kernel(slots, blocks_here, q_ref, kv_ref, idx_ref, bias_ref, causal_ref, o_ref, kbuf, vbuf):
    score_scale = 1.0 / math.sqrt(HEAD_DIM)
    units = bias_ref.shape[0]

    def unit(i, carry):
        head = i // blocks_here
        qblock = i % blocks_here
        for j in range(slots):
            src = pl.multiple_of(idx_ref[i * slots + j] * BLOCK, BLOCK)
            kbuf[pl.ds(j * BLOCK, BLOCK), :] = kv_ref[0, pl.ds(src, BLOCK), :]
            vbuf[pl.ds(j * BLOCK, BLOCK), :] = kv_ref[1, pl.ds(src, BLOCK), :]
        rows = pl.ds(pl.multiple_of(qblock * BLOCK, BLOCK), BLOCK)
        cols = pl.ds(pl.multiple_of(head * HEAD_DIM, HEAD_DIM), HEAD_DIM)
        q = q_ref[rows, cols]
        scores = lax.dot_general(
            q, kbuf[...], (((1,), (1,)), ((), ())), preferred_element_type=jnp.float32
        ) * score_scale
        masked = scores + causal_ref[...] + bias_ref[i]
        top = jnp.max(masked, axis=1, keepdims=True)
        expo = jnp.exp(masked - top)
        denom = jnp.sum(expo, axis=1, keepdims=True)
        out = jnp.dot(expo.astype(jnp.bfloat16), vbuf[...], preferred_element_type=jnp.float32)
        o_ref[rows, cols] = (out / denom).astype(o_ref.dtype)
        return carry

    lax.fori_loop(0, units, unit, 0, unroll=4)


def attend_sparse(queries, keys, values, vertical, slash, block_position):
    row_count = queries.shape[0]
    blocks_here = row_count // BLOCK
    kv_all = lax.all_gather(jnp.stack((keys, values)), "ctx", axis=1, tiled=True)
    index, col_bias, slots = key_block_table(vertical, slash, block_position, blocks_here)
    units = col_bias.shape[0]
    r = lax.broadcasted_iota(jnp.int32, (BLOCK, slots * BLOCK), 0)
    c = lax.broadcasted_iota(jnp.int32, (BLOCK, slots * BLOCK), 1)
    causal_bias = jnp.where((c < BLOCK) & (c > r), NEG_FILL, 0.0).astype(jnp.float32)
    flops = units * 4 * BLOCK * slots * BLOCK * HEAD_DIM
    return pl.pallas_call(
        lambda *refs: sparse_attention_kernel(slots, blocks_here, *refs),
        out_shape=jax.ShapeDtypeStruct(queries.shape, queries.dtype),
        in_specs=[
            pl.BlockSpec(memory_space=pltpu.VMEM),
            pl.BlockSpec(memory_space=pltpu.VMEM),
            pl.BlockSpec(memory_space=pltpu.SMEM),
            pl.BlockSpec(memory_space=pltpu.VMEM),
            pl.BlockSpec(memory_space=pltpu.VMEM),
        ],
        out_specs=pl.BlockSpec(memory_space=pltpu.VMEM),
        scratch_shapes=[
            pltpu.VMEM((slots * BLOCK, HEAD_DIM), jnp.bfloat16),
            pltpu.VMEM((slots * BLOCK, HEAD_DIM), jnp.bfloat16),
        ],
        cost_estimate=pl.CostEstimate(
            flops=flops,
            transcendentals=units * BLOCK * slots * BLOCK,
            bytes_accessed=2 * queries.size * 2 + kv_all.size * 2,
        ),
    )(queries, kv_all, index, col_bias, causal_bias)


SCAN_SHIFTS = (1, 1, 2, 4, 8, 16)


def carry_scan_kernel(x_ref, o_ref, cur, got, send_sems, recv_sems):
    n = lax.axis_size("ctx")
    me = lax.axis_index("ctx")
    tp = lax.axis_index("tp")
    barrier = pltpu.get_barrier_semaphore()
    partners = sorted({k % n for k in SCAN_SHIFTS} | {(-k) % n for k in SCAN_SHIFTS})
    for k in partners:
        pl.semaphore_signal(
            barrier, inc=1, device_id=(lax.rem(me + k, n), tp), device_id_type=pl.DeviceIdType.MESH
        )
    pl.semaphore_wait(barrier, len(partners))
    rounds = len(SCAN_SHIFTS)
    for r, k in enumerate(SCAN_SHIFTS):
        src = x_ref if r == 0 else cur.at[r]
        copy = pltpu.make_async_remote_copy(
            src_ref=src,
            dst_ref=got.at[r],
            send_sem=send_sems.at[r],
            recv_sem=recv_sems.at[r],
            device_id=(lax.rem(me + k, n), tp),
            device_id_type=pl.DeviceIdType.MESH,
        )
        copy.start()
        copy.wait()
        keep = ((me - k + n) // n).astype(jnp.float32)
        incoming = got[r]
        if r == 0:
            new = incoming * keep
        else:
            prev = cur[r]
            decay = prev[0:8]
            new_decay = decay * (incoming[0:8] * keep + (1.0 - keep))
            new_state = prev[8:] + prev[0:1] * (incoming[8:] * keep)
            new = jnp.concatenate([new_decay, new_state], axis=0)
        if r + 1 < rounds:
            cur[r + 1] = new
        else:
            o_ref[...] = new


def carry_scan(packed):
    rounds = len(SCAN_SHIFTS)
    return pl.pallas_call(
        carry_scan_kernel,
        out_shape=jax.ShapeDtypeStruct(packed.shape, packed.dtype),
        in_specs=[pl.BlockSpec(memory_space=pltpu.VMEM)],
        out_specs=pl.BlockSpec(memory_space=pltpu.VMEM),
        scratch_shapes=[
            pltpu.VMEM((rounds,) + packed.shape, packed.dtype),
            pltpu.VMEM((rounds,) + packed.shape, packed.dtype),
            pltpu.SemaphoreType.DMA((rounds,)),
            pltpu.SemaphoreType.DMA((rounds,)),
        ],
        compiler_params=pltpu.CompilerParams(collective_id=0, has_side_effects=True),
    )(packed)


def mamba_mix(ssm_input, gate, state_in, state_out, step_size, decay_log, skip_gain, norm_gain):
    careful = lax.Precision.HIGH
    row_count = ssm_input.shape[0]
    head_count = step_size.shape[1]
    inner_width = ssm_input.shape[1]
    inputs = ssm_input.astype(jnp.float32).reshape(row_count, head_count, SSM_HEAD_DIM)
    in_map = state_in.astype(jnp.float32)
    out_map = state_out.astype(jnp.float32)
    log_steps = -jnp.exp(decay_log)[None, :] * step_size
    cumulative = jnp.cumsum(log_steps, axis=0)
    grouped_per_head = cumulative.T
    lower = jnp.arange(row_count)[:, None] >= jnp.arange(row_count)[None, :]
    decay = jnp.where(
        lower[None],
        jnp.exp(jnp.minimum(grouped_per_head[:, :, None] - grouped_per_head[:, None, :], 0.0)),
        0.0,
    )
    inner = jnp.dot(state_out, state_in.T, preferred_element_type=jnp.float32)
    weighted = inputs * step_size[:, :, None]
    within = jnp.einsum("hts,shp->thp", decay * inner[None], weighted, precision=careful)
    tail = jnp.exp(cumulative[-1][None, :] - cumulative)
    local_state = jnp.einsum(
        "sn,shp->nhp", in_map, weighted * tail[:, :, None], precision=careful
    ).reshape(D_STATE, inner_width)
    carry_decay = jnp.repeat(jnp.exp(cumulative[-1]), SSM_HEAD_DIM)[None, :]

    packed = jnp.concatenate([jnp.broadcast_to(carry_decay, (8, inner_width)), local_state], axis=0)
    incoming = carry_scan(packed)[8:]

    from_past = jnp.dot(
        out_map, incoming, precision=careful, preferred_element_type=jnp.float32
    ).reshape(row_count, head_count, SSM_HEAD_DIM)
    from_past = from_past * jnp.exp(cumulative)[:, :, None]
    mixed = (within + from_past + skip_gain[None, :, None] * inputs).reshape(row_count, inner_width)
    gate_full = gate.astype(jnp.float32)
    gated = mixed * gate_full * jax.nn.sigmoid(gate_full)
    squares = lax.psum(jnp.sum(gated * gated, axis=1), "tp")
    scaled = gated * lax.rsqrt(squares / INNER + 1e-05)[:, None] * norm_gain[None, :]
    return scaled.astype(jnp.bfloat16)


def local(
    queries,
    keys,
    values,
    vertical,
    slash,
    block_position,
    ssm_input,
    gate,
    state_in,
    state_out,
    step_size,
    decay_log,
    skip_gain,
    norm_gain,
):
    attention_out = attend_sparse(queries, keys, values, vertical, slash, block_position)
    recurrent_mixer_result = mamba_mix(
        ssm_input, gate, state_in, state_out, step_size, decay_log, skip_gain, norm_gain
    )
    return (attention_out, recurrent_mixer_result)


def solution(mesh):
    return jax.shard_map(
        local,
        mesh=mesh,
        in_specs=(
            P("ctx", "tp"),
            P("ctx", "tp"),
            P("ctx", "tp"),
            P("tp", None),
            P("tp", None),
            P(),
            P("ctx", "tp"),
            P("ctx", "tp"),
            P("ctx", None),
            P("ctx", None),
            P("ctx", "tp"),
            P("tp"),
            P("tp"),
            P("tp"),
        ),
        out_specs=(P("ctx", "tp"), P("ctx", "tp")),
        check_vma=False,
    )
```

```python
import math

import jax
import jax.numpy as jnp
from jax import lax
from jax.experimental import pallas as pl
from jax.experimental.pallas import tpu as pltpu
from jax.sharding import PartitionSpec as P

HEAD_DIM = 128
SSM_HEAD_DIM = 64
D_STATE = 16
BLOCK = 64
INNER = 16384
NEG_FILL = -1e30


def shifted(array, axis, by):
    size = lax.axis_size(axis)
    pairs = [(i, i + by) for i in range(size) if 0 <= i + by < size]
    return lax.ppermute(array, axis, pairs)


def key_block_table(vertical, slash, block_position, blocks_here):
    my_index = lax.axis_index("ctx")
    total_blocks = block_position.shape[0]
    query_seq = lax.dynamic_slice_in_dim(block_position, my_index * blocks_here, blocks_here)
    heads = vertical.shape[0]
    br = query_seq[None, :, None]
    cand_v = jnp.broadcast_to(vertical[:, None, :], (heads, blocks_here, vertical.shape[1]))
    cand_s = br - slash[:, None, :]
    cand = jnp.concatenate([cand_v, cand_s], axis=-1)
    ok = jnp.concatenate([cand_v < br, cand_s >= 0], axis=-1)
    count = cand.shape[-1]
    earlier = jnp.arange(count)[None, :] < jnp.arange(count)[:, None]
    dup = jnp.any(
        (cand[..., :, None] == cand[..., None, :]) & ok[..., None, :] & earlier[None, None], axis=-1
    )
    ok = ok & ~dup
    diag = jnp.broadcast_to(query_seq[None, :, None], (heads, blocks_here, 1))
    cand = jnp.concatenate([diag, cand, jnp.zeros_like(diag)], axis=-1)
    ok = jnp.concatenate([jnp.ones_like(diag, bool), ok, jnp.zeros_like(diag, bool)], axis=-1)
    match = block_position[None, None, None, :] == cand[..., None]
    index = jnp.sum(jnp.where(match, jnp.arange(total_blocks, dtype=jnp.int32), 0), axis=-1)
    slots = cand.shape[-1]
    col_bias = jnp.where(ok, 0.0, NEG_FILL).astype(jnp.float32)
    col_bias = jnp.repeat(col_bias, BLOCK, axis=-1).reshape(heads * blocks_here, 1, slots * BLOCK)
    return index.reshape(-1).astype(jnp.int32), col_bias, slots


def sparse_attention_kernel(slots, blocks_here, q_ref, kv_ref, idx_ref, bias_ref, causal_ref, o_ref, kbuf, vbuf):
    score_scale = 1.0 / math.sqrt(HEAD_DIM)
    units = bias_ref.shape[0]

    def unit(i, carry):
        head = i // blocks_here
        qblock = i % blocks_here
        for j in range(slots):
            src = pl.multiple_of(idx_ref[i * slots + j] * BLOCK, BLOCK)
            kbuf[pl.ds(j * BLOCK, BLOCK), :] = kv_ref[0, pl.ds(src, BLOCK), :]
            vbuf[pl.ds(j * BLOCK, BLOCK), :] = kv_ref[1, pl.ds(src, BLOCK), :]
        rows = pl.ds(pl.multiple_of(qblock * BLOCK, BLOCK), BLOCK)
        cols = pl.ds(pl.multiple_of(head * HEAD_DIM, HEAD_DIM), HEAD_DIM)
        q = q_ref[rows, cols]
        scores = lax.dot_general(
            q, kbuf[...], (((1,), (1,)), ((), ())), preferred_element_type=jnp.float32
        ) * score_scale
        masked = scores + causal_ref[...] + bias_ref[i]
        top = jnp.max(masked, axis=1, keepdims=True)
        expo = jnp.exp(masked - top)
        denom = jnp.sum(expo, axis=1, keepdims=True)
        out = jnp.dot(expo.astype(jnp.bfloat16), vbuf[...], preferred_element_type=jnp.float32)
        o_ref[rows, cols] = (out / denom).astype(o_ref.dtype)
        return carry

    lax.fori_loop(0, units, unit, 0, unroll=4)


def attend_sparse(queries, keys, values, vertical, slash, block_position):
    row_count = queries.shape[0]
    blocks_here = row_count // BLOCK
    kv_all = lax.all_gather(jnp.stack((keys, values)), "ctx", axis=1, tiled=True)
    index, col_bias, slots = key_block_table(vertical, slash, block_position, blocks_here)
    units = col_bias.shape[0]
    r = lax.broadcasted_iota(jnp.int32, (BLOCK, slots * BLOCK), 0)
    c = lax.broadcasted_iota(jnp.int32, (BLOCK, slots * BLOCK), 1)
    causal_bias = jnp.where((c < BLOCK) & (c > r), NEG_FILL, 0.0).astype(jnp.float32)
    flops = units * 4 * BLOCK * slots * BLOCK * HEAD_DIM
    return pl.pallas_call(
        lambda *refs: sparse_attention_kernel(slots, blocks_here, *refs),
        out_shape=jax.ShapeDtypeStruct(queries.shape, queries.dtype),
        in_specs=[
            pl.BlockSpec(memory_space=pltpu.VMEM),
            pl.BlockSpec(memory_space=pltpu.VMEM),
            pl.BlockSpec(memory_space=pltpu.SMEM),
            pl.BlockSpec(memory_space=pltpu.VMEM),
            pl.BlockSpec(memory_space=pltpu.VMEM),
        ],
        out_specs=pl.BlockSpec(memory_space=pltpu.VMEM),
        scratch_shapes=[
            pltpu.VMEM((slots * BLOCK, HEAD_DIM), jnp.bfloat16),
            pltpu.VMEM((slots * BLOCK, HEAD_DIM), jnp.bfloat16),
        ],
        cost_estimate=pl.CostEstimate(
            flops=flops,
            transcendentals=units * BLOCK * slots * BLOCK,
            bytes_accessed=2 * queries.size * 2 + kv_all.size * 2,
        ),
    )(queries, kv_all, index, col_bias, causal_bias)


SCAN_SHIFTS = (2, 4, 8, 16)


def carry_scan_kernel(s_ref, a_ref, o_ref, cur_s, cur_a, got_s, got_a, sems):
    n = lax.axis_size("ctx")
    me = lax.axis_index("ctx")
    tp = lax.axis_index("tp")
    shifts = (1,) + SCAN_SHIFTS
    barrier = pltpu.get_barrier_semaphore()
    partners = sorted({k % n for k in shifts} | {(-k) % n for k in shifts})
    for k in partners:
        pl.semaphore_signal(
            barrier, inc=1, device_id=(lax.rem(me + k, n), tp), device_id_type=pl.DeviceIdType.MESH
        )
    pl.semaphore_wait(barrier, len(partners))

    def send(slot, k, src_s, src_a):
        target = (lax.rem(me + k, n), tp)
        copies = [
            pltpu.make_async_remote_copy(
                src_ref=src,
                dst_ref=dst.at[slot],
                send_sem=sems.at[part, 0, slot],
                recv_sem=sems.at[part, 1, slot],
                device_id=target,
                device_id_type=pl.DeviceIdType.MESH,
            )
            for part, (src, dst) in enumerate(((src_s, got_s), (src_a, got_a)))
        ]
        for copy in copies:
            copy.start()
        return copies

    def keep_of(k):
        return ((me - k + n) // n).astype(jnp.float32)

    first = send(0, 1, s_ref, a_ref) + send(1, 2, s_ref, a_ref)
    for copy in first:
        copy.wait()
    keep1, keep2 = keep_of(1), keep_of(2)
    a1, a2 = got_a[0], got_a[1]
    state = keep1 * (got_s[0] + a1 * (keep2 * got_s[1]))
    decay = (keep1 * a1 + (1.0 - keep1)) * (keep2 * a2 + (1.0 - keep2))
    for j, k in enumerate(SCAN_SHIFTS):
        cur_s[j] = state
        cur_a[j] = decay
        slot = j + 2
        for copy in send(slot, k, cur_s.at[j], cur_a.at[j]):
            copy.wait()
        keep = keep_of(k)
        state = cur_s[j] + cur_a[j] * (keep * got_s[slot])
        decay = cur_a[j] * (keep * got_a[slot] + (1.0 - keep))
    o_ref[...] = state


def carry_scan(local_state, carry_decay):
    rounds = len(SCAN_SHIFTS)
    slots = rounds + 2
    return pl.pallas_call(
        carry_scan_kernel,
        out_shape=jax.ShapeDtypeStruct(local_state.shape, local_state.dtype),
        in_specs=[pl.BlockSpec(memory_space=pltpu.VMEM)] * 2,
        out_specs=pl.BlockSpec(memory_space=pltpu.VMEM),
        scratch_shapes=[
            pltpu.VMEM((rounds,) + local_state.shape, jnp.float32),
            pltpu.VMEM((rounds,) + carry_decay.shape, jnp.float32),
            pltpu.VMEM((slots,) + local_state.shape, jnp.float32),
            pltpu.VMEM((slots,) + carry_decay.shape, jnp.float32),
            pltpu.SemaphoreType.DMA((2, 2, slots)),
        ],
        compiler_params=pltpu.CompilerParams(collective_id=0, has_side_effects=True),
    )(local_state, carry_decay)


def mamba_mix(ssm_input, gate, state_in, state_out, step_size, decay_log, skip_gain, norm_gain):
    careful = lax.Precision.HIGH
    row_count = ssm_input.shape[0]
    head_count = step_size.shape[1]
    inner_width = ssm_input.shape[1]
    inputs = ssm_input.astype(jnp.float32).reshape(row_count, head_count, SSM_HEAD_DIM)
    in_map = state_in.astype(jnp.float32)
    out_map = state_out.astype(jnp.float32)
    log_steps = -jnp.exp(decay_log)[None, :] * step_size
    cumulative = jnp.cumsum(log_steps, axis=0)
    grouped_per_head = cumulative.T
    lower = jnp.arange(row_count)[:, None] >= jnp.arange(row_count)[None, :]
    decay = jnp.where(
        lower[None],
        jnp.exp(jnp.minimum(grouped_per_head[:, :, None] - grouped_per_head[:, None, :], 0.0)),
        0.0,
    )
    inner = jnp.dot(state_out, state_in.T, preferred_element_type=jnp.float32)
    weighted = inputs * step_size[:, :, None]
    within = jnp.einsum("hts,shp->thp", decay * inner[None], weighted, precision=careful)
    tail = jnp.exp(cumulative[-1][None, :] - cumulative)
    local_state = jnp.einsum(
        "sn,shp->nhp", in_map, weighted * tail[:, :, None], precision=careful
    ).reshape(D_STATE, inner_width)
    carry_decay = jnp.repeat(jnp.exp(cumulative[-1]), SSM_HEAD_DIM)[None, :]

    incoming = carry_scan(local_state, carry_decay)

    from_past = jnp.dot(
        out_map, incoming, precision=careful, preferred_element_type=jnp.float32
    ).reshape(row_count, head_count, SSM_HEAD_DIM)
    from_past = from_past * jnp.exp(cumulative)[:, :, None]
    mixed = (within + from_past + skip_gain[None, :, None] * inputs).reshape(row_count, inner_width)
    gate_full = gate.astype(jnp.float32)
    gated = mixed * gate_full * jax.nn.sigmoid(gate_full)
    squares = lax.psum(jnp.sum(gated * gated, axis=1), "tp")
    scaled = gated * lax.rsqrt(squares / INNER + 1e-05)[:, None] * norm_gain[None, :]
    return scaled.astype(jnp.bfloat16)


def local(
    queries,
    keys,
    values,
    vertical,
    slash,
    block_position,
    ssm_input,
    gate,
    state_in,
    state_out,
    step_size,
    decay_log,
    skip_gain,
    norm_gain,
):
    attention_out = attend_sparse(queries, keys, values, vertical, slash, block_position)
    recurrent_mixer_result = mamba_mix(
        ssm_input, gate, state_in, state_out, step_size, decay_log, skip_gain, norm_gain
    )
    return (attention_out, recurrent_mixer_result)


def solution(mesh):
    return jax.shard_map(
        local,
        mesh=mesh,
        in_specs=(
            P("ctx", "tp"),
            P("ctx", "tp"),
            P("ctx", "tp"),
            P("tp", None),
            P("tp", None),
            P(),
            P("ctx", "tp"),
            P("ctx", "tp"),
            P("ctx", None),
            P("ctx", None),
            P("ctx", "tp"),
            P("tp"),
            P("tp"),
            P("tp"),
        ),
        out_specs=(P("ctx", "tp"), P("ctx", "tp")),
        check_vma=False,
    )
```

```python
import math

import jax
import jax.numpy as jnp
from jax import lax
from jax.experimental import pallas as pl
from jax.experimental.pallas import tpu as pltpu
from jax.sharding import PartitionSpec as P

HEAD_DIM = 128
SSM_HEAD_DIM = 64
D_STATE = 16
BLOCK = 64
INNER = 16384
NEG_FILL = -1e30


def shifted(array, axis, by):
    size = lax.axis_size(axis)
    pairs = [(i, i + by) for i in range(size) if 0 <= i + by < size]
    return lax.ppermute(array, axis, pairs)


def key_block_table(vertical, slash, block_position, blocks_here):
    my_index = lax.axis_index("ctx")
    total_blocks = block_position.shape[0]
    query_seq = lax.dynamic_slice_in_dim(block_position, my_index * blocks_here, blocks_here)
    heads = vertical.shape[0]
    br = query_seq[None, :, None]
    cand_v = jnp.broadcast_to(vertical[:, None, :], (heads, blocks_here, vertical.shape[1]))
    cand_s = br - slash[:, None, :]
    cand = jnp.concatenate([cand_v, cand_s], axis=-1)
    ok = jnp.concatenate([cand_v < br, cand_s >= 0], axis=-1)
    count = cand.shape[-1]
    earlier = jnp.arange(count)[None, :] < jnp.arange(count)[:, None]
    dup = jnp.any(
        (cand[..., :, None] == cand[..., None, :]) & ok[..., None, :] & earlier[None, None], axis=-1
    )
    ok = ok & ~dup
    diag = jnp.broadcast_to(query_seq[None, :, None], (heads, blocks_here, 1))
    cand = jnp.concatenate([diag, cand, jnp.zeros_like(diag)], axis=-1)
    ok = jnp.concatenate([jnp.ones_like(diag, bool), ok, jnp.zeros_like(diag, bool)], axis=-1)
    match = block_position[None, None, None, :] == cand[..., None]
    index = jnp.sum(jnp.where(match, jnp.arange(total_blocks, dtype=jnp.int32), 0), axis=-1)
    slots = cand.shape[-1]
    col_bias = jnp.where(ok, 0.0, NEG_FILL).astype(jnp.float32)
    col_bias = jnp.repeat(col_bias, BLOCK, axis=-1).reshape(heads * blocks_here, 1, slots * BLOCK)
    return index.reshape(-1).astype(jnp.int32), col_bias, slots


def sparse_attention_kernel(slots, blocks_here, q_ref, kv_ref, idx_ref, bias_ref, causal_ref, o_ref, kbuf, vbuf):
    score_scale = 1.0 / math.sqrt(HEAD_DIM)
    units = bias_ref.shape[0]

    def unit(i, carry):
        head = i // blocks_here
        qblock = i % blocks_here
        for j in range(slots):
            src = pl.multiple_of(idx_ref[i * slots + j] * BLOCK, BLOCK)
            kbuf[pl.ds(j * BLOCK, BLOCK), :] = kv_ref[0, pl.ds(src, BLOCK), :]
            vbuf[pl.ds(j * BLOCK, BLOCK), :] = kv_ref[1, pl.ds(src, BLOCK), :]
        rows = pl.ds(pl.multiple_of(qblock * BLOCK, BLOCK), BLOCK)
        cols = pl.ds(pl.multiple_of(head * HEAD_DIM, HEAD_DIM), HEAD_DIM)
        q = q_ref[rows, cols]
        scores = lax.dot_general(
            q, kbuf[...], (((1,), (1,)), ((), ())), preferred_element_type=jnp.float32
        ) * score_scale
        masked = scores + causal_ref[...] + bias_ref[i]
        top = jnp.max(masked, axis=1, keepdims=True)
        expo = jnp.exp(masked - top)
        denom = jnp.sum(expo, axis=1, keepdims=True)
        out = jnp.dot(expo.astype(jnp.bfloat16), vbuf[...], preferred_element_type=jnp.float32)
        o_ref[rows, cols] = (out / denom).astype(o_ref.dtype)
        return carry

    lax.fori_loop(0, units, unit, 0, unroll=units)


def attend_sparse(queries, keys, values, vertical, slash, block_position):
    row_count = queries.shape[0]
    blocks_here = row_count // BLOCK
    kv_all = lax.all_gather(jnp.stack((keys, values)), "ctx", axis=1, tiled=True)
    index, col_bias, slots = key_block_table(vertical, slash, block_position, blocks_here)
    units = col_bias.shape[0]
    r = lax.broadcasted_iota(jnp.int32, (BLOCK, slots * BLOCK), 0)
    c = lax.broadcasted_iota(jnp.int32, (BLOCK, slots * BLOCK), 1)
    causal_bias = jnp.where((c < BLOCK) & (c > r), NEG_FILL, 0.0).astype(jnp.float32)
    flops = units * 4 * BLOCK * slots * BLOCK * HEAD_DIM
    return pl.pallas_call(
        lambda *refs: sparse_attention_kernel(slots, blocks_here, *refs),
        out_shape=jax.ShapeDtypeStruct(queries.shape, queries.dtype),
        in_specs=[
            pl.BlockSpec(memory_space=pltpu.VMEM),
            pl.BlockSpec(memory_space=pltpu.VMEM),
            pl.BlockSpec(memory_space=pltpu.SMEM),
            pl.BlockSpec(memory_space=pltpu.VMEM),
            pl.BlockSpec(memory_space=pltpu.VMEM),
        ],
        out_specs=pl.BlockSpec(memory_space=pltpu.VMEM),
        scratch_shapes=[
            pltpu.VMEM((slots * BLOCK, HEAD_DIM), jnp.bfloat16),
            pltpu.VMEM((slots * BLOCK, HEAD_DIM), jnp.bfloat16),
        ],
        cost_estimate=pl.CostEstimate(
            flops=flops,
            transcendentals=units * BLOCK * slots * BLOCK,
            bytes_accessed=2 * queries.size * 2 + kv_all.size * 2,
        ),
    )(queries, kv_all, index, col_bias, causal_bias)


SCAN_SHIFTS = (2, 4, 8, 16)


def carry_scan_kernel(s_ref, a_ref, o_ref, cur_s, cur_a, got_s, got_a, sems):
    n = lax.axis_size("ctx")
    me = lax.axis_index("ctx")
    tp = lax.axis_index("tp")
    shifts = (1,) + SCAN_SHIFTS
    barrier = pltpu.get_barrier_semaphore()
    partners = sorted({k % n for k in shifts} | {(-k) % n for k in shifts})
    for k in partners:
        pl.semaphore_signal(
            barrier, inc=1, device_id=(lax.rem(me + k, n), tp), device_id_type=pl.DeviceIdType.MESH
        )
    pl.semaphore_wait(barrier, len(partners))

    def send(slot, k, src_s, src_a):
        target = (lax.rem(me + k, n), tp)
        copies = [
            pltpu.make_async_remote_copy(
                src_ref=src,
                dst_ref=dst.at[slot],
                send_sem=sems.at[part, 0, slot],
                recv_sem=sems.at[part, 1, slot],
                device_id=target,
                device_id_type=pl.DeviceIdType.MESH,
            )
            for part, (src, dst) in enumerate(((src_s, got_s), (src_a, got_a)))
        ]
        for copy in copies:
            copy.start()
        return copies

    def keep_of(k):
        return ((me - k + n) // n).astype(jnp.float32)

    first = send(0, 1, s_ref, a_ref) + send(1, 2, s_ref, a_ref)
    for copy in first:
        copy.wait()
    keep1, keep2 = keep_of(1), keep_of(2)
    a1, a2 = got_a[0], got_a[1]
    state = keep1 * (got_s[0] + a1 * (keep2 * got_s[1]))
    decay = (keep1 * a1 + (1.0 - keep1)) * (keep2 * a2 + (1.0 - keep2))
    for j, k in enumerate(SCAN_SHIFTS):
        cur_s[j] = state
        cur_a[j] = decay
        slot = j + 2
        for copy in send(slot, k, cur_s.at[j], cur_a.at[j]):
            copy.wait()
        keep = keep_of(k)
        state = cur_s[j] + cur_a[j] * (keep * got_s[slot])
        decay = cur_a[j] * (keep * got_a[slot] + (1.0 - keep))
    o_ref[...] = state


def carry_scan(local_state, carry_decay):
    rounds = len(SCAN_SHIFTS)
    slots = rounds + 2
    return pl.pallas_call(
        carry_scan_kernel,
        out_shape=jax.ShapeDtypeStruct(local_state.shape, local_state.dtype),
        in_specs=[pl.BlockSpec(memory_space=pltpu.VMEM)] * 2,
        out_specs=pl.BlockSpec(memory_space=pltpu.VMEM),
        scratch_shapes=[
            pltpu.VMEM((rounds,) + local_state.shape, jnp.float32),
            pltpu.VMEM((rounds,) + carry_decay.shape, jnp.float32),
            pltpu.VMEM((slots,) + local_state.shape, jnp.float32),
            pltpu.VMEM((slots,) + carry_decay.shape, jnp.float32),
            pltpu.SemaphoreType.DMA((2, 2, slots)),
        ],
        compiler_params=pltpu.CompilerParams(collective_id=0, has_side_effects=True),
    )(local_state, carry_decay)


def mamba_mix(ssm_input, gate, state_in, state_out, step_size, decay_log, skip_gain, norm_gain):
    careful = lax.Precision.HIGH
    row_count = ssm_input.shape[0]
    head_count = step_size.shape[1]
    inner_width = ssm_input.shape[1]
    inputs = ssm_input.astype(jnp.float32).reshape(row_count, head_count, SSM_HEAD_DIM)
    in_map = state_in.astype(jnp.float32)
    out_map = state_out.astype(jnp.float32)
    log_steps = -jnp.exp(decay_log)[None, :] * step_size
    cumulative = jnp.cumsum(log_steps, axis=0)
    grouped_per_head = cumulative.T
    lower = jnp.arange(row_count)[:, None] >= jnp.arange(row_count)[None, :]
    decay = jnp.where(
        lower[None],
        jnp.exp(jnp.minimum(grouped_per_head[:, :, None] - grouped_per_head[:, None, :], 0.0)),
        0.0,
    )
    inner = jnp.dot(state_out, state_in.T, preferred_element_type=jnp.float32)
    weighted = inputs * step_size[:, :, None]
    within = jnp.einsum("hts,shp->thp", decay * inner[None], weighted, precision=careful)
    tail = jnp.exp(cumulative[-1][None, :] - cumulative)
    local_state = jnp.einsum(
        "sn,shp->nhp", in_map, weighted * tail[:, :, None], precision=careful
    ).reshape(D_STATE, inner_width)
    carry_decay = jnp.repeat(jnp.exp(cumulative[-1]), SSM_HEAD_DIM)[None, :]

    incoming = carry_scan(local_state, carry_decay)

    from_past = jnp.dot(
        out_map, incoming, precision=careful, preferred_element_type=jnp.float32
    ).reshape(row_count, head_count, SSM_HEAD_DIM)
    from_past = from_past * jnp.exp(cumulative)[:, :, None]
    mixed = (within + from_past + skip_gain[None, :, None] * inputs).reshape(row_count, inner_width)
    gate_full = gate.astype(jnp.float32)
    gated = mixed * gate_full * jax.nn.sigmoid(gate_full)
    squares = lax.psum(jnp.sum(gated * gated, axis=1), "tp")
    scaled = gated * lax.rsqrt(squares / INNER + 1e-05)[:, None] * norm_gain[None, :]
    return scaled.astype(jnp.bfloat16)


def local(
    queries,
    keys,
    values,
    vertical,
    slash,
    block_position,
    ssm_input,
    gate,
    state_in,
    state_out,
    step_size,
    decay_log,
    skip_gain,
    norm_gain,
):
    attention_out = attend_sparse(queries, keys, values, vertical, slash, block_position)
    recurrent_mixer_result = mamba_mix(
        ssm_input, gate, state_in, state_out, step_size, decay_log, skip_gain, norm_gain
    )
    return (attention_out, recurrent_mixer_result)


def solution(mesh):
    return jax.shard_map(
        local,
        mesh=mesh,
        in_specs=(
            P("ctx", "tp"),
            P("ctx", "tp"),
            P("ctx", "tp"),
            P("tp", None),
            P("tp", None),
            P(),
            P("ctx", "tp"),
            P("ctx", "tp"),
            P("ctx", None),
            P("ctx", None),
            P("ctx", "tp"),
            P("tp"),
            P("tp"),
            P("tp"),
        ),
        out_specs=(P("ctx", "tp"), P("ctx", "tp")),
        check_vma=False,
    )
```

```python
import math

import jax
import jax.numpy as jnp
from jax import lax
from jax.experimental import pallas as pl
from jax.experimental.pallas import tpu as pltpu
from jax.sharding import PartitionSpec as P

HEAD_DIM = 128
SSM_HEAD_DIM = 64
D_STATE = 16
BLOCK = 64
INNER = 16384
NEG_FILL = -1e30


def shifted(array, axis, by):
    size = lax.axis_size(axis)
    pairs = [(i, i + by) for i in range(size) if 0 <= i + by < size]
    return lax.ppermute(array, axis, pairs)


def key_block_table(vertical, slash, block_position, blocks_here):
    my_index = lax.axis_index("ctx")
    total_blocks = block_position.shape[0]
    query_seq = lax.dynamic_slice_in_dim(block_position, my_index * blocks_here, blocks_here)
    heads = vertical.shape[0]
    br = query_seq[None, :, None]
    cand_v = jnp.broadcast_to(vertical[:, None, :], (heads, blocks_here, vertical.shape[1]))
    cand_s = br - slash[:, None, :]
    cand = jnp.concatenate([cand_v, cand_s], axis=-1)
    ok = jnp.concatenate([cand_v < br, cand_s >= 0], axis=-1)
    count = cand.shape[-1]
    earlier = jnp.arange(count)[None, :] < jnp.arange(count)[:, None]
    dup = jnp.any(
        (cand[..., :, None] == cand[..., None, :]) & ok[..., None, :] & earlier[None, None], axis=-1
    )
    ok = ok & ~dup
    diag = jnp.broadcast_to(query_seq[None, :, None], (heads, blocks_here, 1))
    cand = jnp.concatenate([diag, cand, jnp.zeros_like(diag)], axis=-1)
    ok = jnp.concatenate([jnp.ones_like(diag, bool), ok, jnp.zeros_like(diag, bool)], axis=-1)
    match = block_position[None, None, None, :] == cand[..., None]
    index = jnp.sum(jnp.where(match, jnp.arange(total_blocks, dtype=jnp.int32), 0), axis=-1)
    slots = cand.shape[-1]
    col_bias = jnp.where(ok, 0.0, NEG_FILL).astype(jnp.float32)
    col_bias = jnp.repeat(col_bias, BLOCK, axis=-1).reshape(heads * blocks_here, 1, slots * BLOCK)
    return index.reshape(-1).astype(jnp.int32), col_bias, slots


def sparse_attention_kernel(slots, blocks_here, q_ref, kv_ref, idx_ref, bias_ref, causal_ref, o_ref, kbuf, vbuf):
    score_scale = 1.0 / math.sqrt(HEAD_DIM)
    units = bias_ref.shape[0]

    def unit(i, carry):
        head = i // blocks_here
        qblock = i % blocks_here
        for j in range(slots):
            src = pl.multiple_of(idx_ref[i * slots + j] * BLOCK, BLOCK)
            kbuf[pl.ds(j * BLOCK, BLOCK), :] = kv_ref[0, pl.ds(src, BLOCK), :]
            vbuf[pl.ds(j * BLOCK, BLOCK), :] = kv_ref[1, pl.ds(src, BLOCK), :]
        rows = pl.ds(pl.multiple_of(qblock * BLOCK, BLOCK), BLOCK)
        cols = pl.ds(pl.multiple_of(head * HEAD_DIM, HEAD_DIM), HEAD_DIM)
        q = q_ref[rows, cols]
        scores = lax.dot_general(
            q, kbuf[...], (((1,), (1,)), ((), ())), preferred_element_type=jnp.float32
        ) * score_scale
        masked = scores + causal_ref[...] + bias_ref[i]
        top = jnp.max(masked, axis=1, keepdims=True)
        expo = jnp.exp(masked - top)
        denom = jnp.sum(expo, axis=1, keepdims=True)
        out = jnp.dot(expo.astype(jnp.bfloat16), vbuf[...], preferred_element_type=jnp.float32)
        o_ref[rows, cols] = (out / denom).astype(o_ref.dtype)
        return carry

    lax.fori_loop(0, units, unit, 0, unroll=units)


def attend_sparse(queries, kv_local, vertical, slash, block_position):
    row_count = queries.shape[0]
    blocks_here = row_count // BLOCK
    kv_all = lax.all_gather(kv_local, "ctx", axis=1, tiled=True)
    index, col_bias, slots = key_block_table(vertical, slash, block_position, blocks_here)
    units = col_bias.shape[0]
    r = lax.broadcasted_iota(jnp.int32, (BLOCK, slots * BLOCK), 0)
    c = lax.broadcasted_iota(jnp.int32, (BLOCK, slots * BLOCK), 1)
    causal_bias = jnp.where((c < BLOCK) & (c > r), NEG_FILL, 0.0).astype(jnp.float32)
    flops = units * 4 * BLOCK * slots * BLOCK * HEAD_DIM
    return pl.pallas_call(
        lambda *refs: sparse_attention_kernel(slots, blocks_here, *refs),
        out_shape=jax.ShapeDtypeStruct(queries.shape, queries.dtype),
        in_specs=[
            pl.BlockSpec(memory_space=pltpu.VMEM),
            pl.BlockSpec(memory_space=pltpu.VMEM),
            pl.BlockSpec(memory_space=pltpu.SMEM),
            pl.BlockSpec(memory_space=pltpu.VMEM),
            pl.BlockSpec(memory_space=pltpu.VMEM),
        ],
        out_specs=pl.BlockSpec(memory_space=pltpu.VMEM),
        scratch_shapes=[
            pltpu.VMEM((slots * BLOCK, HEAD_DIM), jnp.bfloat16),
            pltpu.VMEM((slots * BLOCK, HEAD_DIM), jnp.bfloat16),
        ],
        cost_estimate=pl.CostEstimate(
            flops=flops,
            transcendentals=units * BLOCK * slots * BLOCK,
            bytes_accessed=2 * queries.size * 2 + kv_all.size * 2,
        ),
    )(queries, kv_all, index, col_bias, causal_bias)


SCAN_SHIFTS = (2, 4, 8, 16)


def carry_scan_kernel(s_ref, a_ref, o_ref, cur_s, cur_a, got_s, got_a, sems):
    n = lax.axis_size("ctx")
    me = lax.axis_index("ctx")
    tp = lax.axis_index("tp")
    shifts = (1,) + SCAN_SHIFTS
    barrier = pltpu.get_barrier_semaphore()
    partners = sorted({k % n for k in shifts} | {(-k) % n for k in shifts})
    for k in partners:
        pl.semaphore_signal(
            barrier, inc=1, device_id=(lax.rem(me + k, n), tp), device_id_type=pl.DeviceIdType.MESH
        )
    pl.semaphore_wait(barrier, len(partners))

    def send(slot, k, src_s, src_a):
        target = (lax.rem(me + k, n), tp)
        copies = [
            pltpu.make_async_remote_copy(
                src_ref=src,
                dst_ref=dst.at[slot],
                send_sem=sems.at[part, 0, slot],
                recv_sem=sems.at[part, 1, slot],
                device_id=target,
                device_id_type=pl.DeviceIdType.MESH,
            )
            for part, (src, dst) in enumerate(((src_s, got_s), (src_a, got_a)))
        ]
        for copy in copies:
            copy.start()
        return copies

    def keep_of(k):
        return ((me - k + n) // n).astype(jnp.float32)

    first = send(0, 1, s_ref, a_ref) + send(1, 2, s_ref, a_ref)
    for copy in first:
        copy.wait()
    keep1, keep2 = keep_of(1), keep_of(2)
    a1, a2 = got_a[0], got_a[1]
    state = keep1 * (got_s[0] + a1 * (keep2 * got_s[1]))
    decay = (keep1 * a1 + (1.0 - keep1)) * (keep2 * a2 + (1.0 - keep2))
    for j, k in enumerate(SCAN_SHIFTS):
        cur_s[j] = state
        cur_a[j] = decay
        slot = j + 2
        for copy in send(slot, k, cur_s.at[j], cur_a.at[j]):
            copy.wait()
        keep = keep_of(k)
        state = cur_s[j] + cur_a[j] * (keep * got_s[slot])
        decay = cur_a[j] * (keep * got_a[slot] + (1.0 - keep))
    o_ref[...] = state


def carry_scan(local_state, carry_decay):
    rounds = len(SCAN_SHIFTS)
    slots = rounds + 2
    return pl.pallas_call(
        carry_scan_kernel,
        out_shape=jax.ShapeDtypeStruct(local_state.shape, local_state.dtype),
        in_specs=[pl.BlockSpec(memory_space=pltpu.VMEM)] * 2,
        out_specs=pl.BlockSpec(memory_space=pltpu.VMEM),
        scratch_shapes=[
            pltpu.VMEM((rounds,) + local_state.shape, jnp.float32),
            pltpu.VMEM((rounds,) + carry_decay.shape, jnp.float32),
            pltpu.VMEM((slots,) + local_state.shape, jnp.float32),
            pltpu.VMEM((slots,) + carry_decay.shape, jnp.float32),
            pltpu.SemaphoreType.DMA((2, 2, slots)),
        ],
        compiler_params=pltpu.CompilerParams(collective_id=0, has_side_effects=True),
    )(local_state, carry_decay)


def tp_sum_kernel(x_ref, o_ref, got, sems):
    n = lax.axis_size("tp")
    me = lax.axis_index("tp")
    row = lax.axis_index("ctx")
    barrier = pltpu.get_barrier_semaphore()
    for k in range(1, n):
        pl.semaphore_signal(
            barrier, inc=1, device_id=(row, lax.rem(me + k, n)), device_id_type=pl.DeviceIdType.MESH
        )
    pl.semaphore_wait(barrier, n - 1)
    copies = []
    for k in range(1, n):
        copy = pltpu.make_async_remote_copy(
            src_ref=x_ref,
            dst_ref=got.at[me],
            send_sem=sems.at[0, k],
            recv_sem=sems.at[1, k],
            device_id=(row, lax.rem(me + k, n)),
            device_id_type=pl.DeviceIdType.MESH,
        )
        copy.start()
        copies.append(copy)
    got[me] = x_ref[...]
    for k in range(1, n):
        copies[k - 1].wait_send()
        arriving = pltpu.make_async_remote_copy(
            src_ref=x_ref,
            dst_ref=got.at[lax.rem(me - k + n, n)],
            send_sem=sems.at[0, k],
            recv_sem=sems.at[1, k],
            device_id=(row, lax.rem(me + k, n)),
            device_id_type=pl.DeviceIdType.MESH,
        )
        arriving.wait_recv()
    total = got[0]
    for j in range(1, n):
        total = total + got[j]
    o_ref[...] = total


def tp_sum(values):
    n = lax.axis_size("tp")
    rows = values.size // 128
    shaped = jnp.pad(values.reshape(rows, 128), ((0, (-rows) % 8), (0, 0)))
    out = pl.pallas_call(
        tp_sum_kernel,
        out_shape=jax.ShapeDtypeStruct(shaped.shape, shaped.dtype),
        in_specs=[pl.BlockSpec(memory_space=pltpu.VMEM)],
        out_specs=pl.BlockSpec(memory_space=pltpu.VMEM),
        scratch_shapes=[
            pltpu.VMEM((n,) + shaped.shape, shaped.dtype),
            pltpu.SemaphoreType.DMA((2, n)),
        ],
        compiler_params=pltpu.CompilerParams(collective_id=1, has_side_effects=True),
    )(shaped)
    return out.reshape(-1)[: values.size]


def mamba_mix(ssm_input, gate, state_in, state_out, step_size, decay_log, skip_gain, norm_gain):
    careful = lax.Precision.HIGH
    row_count = ssm_input.shape[0]
    head_count = step_size.shape[1]
    inner_width = ssm_input.shape[1]
    inputs = ssm_input.astype(jnp.float32).reshape(row_count, head_count, SSM_HEAD_DIM)
    in_map = state_in.astype(jnp.float32)
    out_map = state_out.astype(jnp.float32)
    log_steps = -jnp.exp(decay_log)[None, :] * step_size
    cumulative = jnp.cumsum(log_steps, axis=0)
    grouped_per_head = cumulative.T
    lower = jnp.arange(row_count)[:, None] >= jnp.arange(row_count)[None, :]
    decay = jnp.where(
        lower[None],
        jnp.exp(jnp.minimum(grouped_per_head[:, :, None] - grouped_per_head[:, None, :], 0.0)),
        0.0,
    )
    inner = jnp.dot(state_out, state_in.T, preferred_element_type=jnp.float32)
    weighted = inputs * step_size[:, :, None]
    within = jnp.einsum("hts,shp->thp", decay * inner[None], weighted, precision=careful)
    tail = jnp.exp(cumulative[-1][None, :] - cumulative)
    local_state = jnp.einsum(
        "sn,shp->nhp", in_map, weighted * tail[:, :, None], precision=careful
    ).reshape(D_STATE, inner_width)
    carry_decay = jnp.repeat(jnp.exp(cumulative[-1]), SSM_HEAD_DIM)[None, :]

    incoming = carry_scan(local_state, carry_decay)

    from_past = jnp.dot(
        out_map, incoming, precision=careful, preferred_element_type=jnp.float32
    ).reshape(row_count, head_count, SSM_HEAD_DIM)
    from_past = from_past * jnp.exp(cumulative)[:, :, None]
    mixed = (within + from_past + skip_gain[None, :, None] * inputs).reshape(row_count, inner_width)
    gate_full = gate.astype(jnp.float32)
    gated = mixed * gate_full * jax.nn.sigmoid(gate_full)
    squares = tp_sum(jnp.sum(gated * gated, axis=1))
    scaled = gated * lax.rsqrt(squares / INNER + 1e-05)[:, None] * norm_gain[None, :]
    return scaled.astype(jnp.bfloat16)


def local(
    queries,
    keys,
    values,
    vertical,
    slash,
    block_position,
    ssm_input,
    gate,
    state_in,
    state_out,
    step_size,
    decay_log,
    skip_gain,
    norm_gain,
):
    kv_local = jnp.stack((keys, values))
    kv_local, ssm_input, step_size, decay_log, state_in = lax.optimization_barrier(
        (kv_local, ssm_input, step_size, decay_log, state_in)
    )
    attention_out = attend_sparse(queries, kv_local, vertical, slash, block_position)
    recurrent_mixer_result = mamba_mix(
        ssm_input, gate, state_in, state_out, step_size, decay_log, skip_gain, norm_gain
    )
    return (attention_out, recurrent_mixer_result)


def solution(mesh):
    return jax.shard_map(
        local,
        mesh=mesh,
        in_specs=(
            P("ctx", "tp"),
            P("ctx", "tp"),
            P("ctx", "tp"),
            P("tp", None),
            P("tp", None),
            P(),
            P("ctx", "tp"),
            P("ctx", "tp"),
            P("ctx", None),
            P("ctx", None),
            P("ctx", "tp"),
            P("tp"),
            P("tp"),
            P("tp"),
        ),
        out_specs=(P("ctx", "tp"), P("ctx", "tp")),
        check_vma=False,
    )
```

```python
import math

import jax
import jax.numpy as jnp
from jax import lax
from jax.experimental import pallas as pl
from jax.experimental.pallas import tpu as pltpu
from jax.sharding import PartitionSpec as P

HEAD_DIM = 128
SSM_HEAD_DIM = 64
D_STATE = 16
BLOCK = 64
INNER = 16384
NEG_FILL = -1e30


def shifted(array, axis, by):
    size = lax.axis_size(axis)
    pairs = [(i, i + by) for i in range(size) if 0 <= i + by < size]
    return lax.ppermute(array, axis, pairs)


def key_block_table(vertical, slash, block_position, blocks_here):
    my_index = lax.axis_index("ctx")
    total_blocks = block_position.shape[0]
    query_seq = lax.dynamic_slice_in_dim(block_position, my_index * blocks_here, blocks_here)
    heads = vertical.shape[0]
    br = query_seq[None, :, None]
    cand_v = jnp.broadcast_to(vertical[:, None, :], (heads, blocks_here, vertical.shape[1]))
    cand_s = br - slash[:, None, :]
    cand = jnp.concatenate([cand_v, cand_s], axis=-1)
    ok = jnp.concatenate([cand_v < br, cand_s >= 0], axis=-1)
    count = cand.shape[-1]
    earlier = jnp.arange(count)[None, :] < jnp.arange(count)[:, None]
    dup = jnp.any(
        (cand[..., :, None] == cand[..., None, :]) & ok[..., None, :] & earlier[None, None], axis=-1
    )
    ok = ok & ~dup
    diag = jnp.broadcast_to(query_seq[None, :, None], (heads, blocks_here, 1))
    cand = jnp.concatenate([diag, cand, jnp.zeros_like(diag)], axis=-1)
    ok = jnp.concatenate([jnp.ones_like(diag, bool), ok, jnp.zeros_like(diag, bool)], axis=-1)
    match = block_position[None, None, None, :] == cand[..., None]
    index = jnp.sum(jnp.where(match, jnp.arange(total_blocks, dtype=jnp.int32), 0), axis=-1)
    slots = cand.shape[-1]
    col_bias = jnp.where(ok, 0.0, NEG_FILL).astype(jnp.float32)
    col_bias = jnp.repeat(col_bias, BLOCK, axis=-1).reshape(heads * blocks_here, 1, slots * BLOCK)
    return index.reshape(-1).astype(jnp.int32), col_bias, slots


def sparse_attention_kernel(slots, blocks_here, q_ref, kv_ref, idx_ref, bias_ref, causal_ref, o_ref, kbuf, vbuf):
    score_scale = 1.0 / math.sqrt(HEAD_DIM)
    units = bias_ref.shape[0]

    def unit(i, carry):
        head = i // blocks_here
        qblock = i % blocks_here
        for j in range(slots):
            src = pl.multiple_of(idx_ref[i * slots + j] * BLOCK, BLOCK)
            kbuf[pl.ds(j * BLOCK, BLOCK), :] = kv_ref[0, pl.ds(src, BLOCK), :]
            vbuf[pl.ds(j * BLOCK, BLOCK), :] = kv_ref[1, pl.ds(src, BLOCK), :]
        rows = pl.ds(pl.multiple_of(qblock * BLOCK, BLOCK), BLOCK)
        cols = pl.ds(pl.multiple_of(head * HEAD_DIM, HEAD_DIM), HEAD_DIM)
        q = q_ref[rows, cols]
        scores = lax.dot_general(
            q, kbuf[...], (((1,), (1,)), ((), ())), preferred_element_type=jnp.float32
        ) * score_scale
        masked = scores + causal_ref[...] + bias_ref[i]
        top = jnp.max(masked, axis=1, keepdims=True)
        expo = jnp.exp(masked - top)
        denom = jnp.sum(expo, axis=1, keepdims=True)
        out = jnp.dot(expo.astype(jnp.bfloat16), vbuf[...], preferred_element_type=jnp.float32)
        o_ref[rows, cols] = (out / denom).astype(o_ref.dtype)
        return carry

    lax.fori_loop(0, units, unit, 0, unroll=units)


def attend_sparse(queries, kv_local, vertical, slash, block_position):
    row_count = queries.shape[0]
    blocks_here = row_count // BLOCK
    kv_all = lax.all_gather(kv_local, "ctx", axis=1, tiled=True)
    index, col_bias, slots = key_block_table(vertical, slash, block_position, blocks_here)
    units = col_bias.shape[0]
    r = lax.broadcasted_iota(jnp.int32, (BLOCK, slots * BLOCK), 0)
    c = lax.broadcasted_iota(jnp.int32, (BLOCK, slots * BLOCK), 1)
    causal_bias = jnp.where((c < BLOCK) & (c > r), NEG_FILL, 0.0).astype(jnp.float32)
    flops = units * 4 * BLOCK * slots * BLOCK * HEAD_DIM
    return pl.pallas_call(
        lambda *refs: sparse_attention_kernel(slots, blocks_here, *refs),
        out_shape=jax.ShapeDtypeStruct(queries.shape, queries.dtype),
        in_specs=[
            pl.BlockSpec(memory_space=pltpu.VMEM),
            pl.BlockSpec(memory_space=pltpu.VMEM),
            pl.BlockSpec(memory_space=pltpu.SMEM),
            pl.BlockSpec(memory_space=pltpu.VMEM),
            pl.BlockSpec(memory_space=pltpu.VMEM),
        ],
        out_specs=pl.BlockSpec(memory_space=pltpu.VMEM),
        scratch_shapes=[
            pltpu.VMEM((slots * BLOCK, HEAD_DIM), jnp.bfloat16),
            pltpu.VMEM((slots * BLOCK, HEAD_DIM), jnp.bfloat16),
        ],
        cost_estimate=pl.CostEstimate(
            flops=flops,
            transcendentals=units * BLOCK * slots * BLOCK,
            bytes_accessed=2 * queries.size * 2 + kv_all.size * 2,
        ),
    )(queries, kv_all, index, col_bias, causal_bias)


SCAN_ROUNDS = ((1, 2, 3, 4), (4, 8, 12), (16,))


def carry_scan_kernel(s_ref, a_ref, o_ref, cur_s, cur_a, got_s, got_a, sems):
    n = lax.axis_size("ctx")
    me = lax.axis_index("ctx")
    tp = lax.axis_index("tp")
    shifts = [k for ks in SCAN_ROUNDS for k in ks]
    barrier = pltpu.get_barrier_semaphore()
    partners = sorted({k % n for k in shifts} | {(-k) % n for k in shifts})
    for k in partners:
        pl.semaphore_signal(
            barrier, inc=1, device_id=(lax.rem(me + k, n), tp), device_id_type=pl.DeviceIdType.MESH
        )
    pl.semaphore_wait(barrier, len(partners))

    def send(slot, k, src_s, src_a):
        target = (lax.rem(me + k, n), tp)
        copies = [
            pltpu.make_async_remote_copy(
                src_ref=src,
                dst_ref=dst.at[slot],
                send_sem=sems.at[part, 0, slot],
                recv_sem=sems.at[part, 1, slot],
                device_id=target,
                device_id_type=pl.DeviceIdType.MESH,
            )
            for part, (src, dst) in enumerate(((src_s, got_s), (src_a, got_a)))
        ]
        for copy in copies:
            copy.start()
        return copies

    def arrived(slot, k):
        keep = ((me - k + n) // n).astype(jnp.float32)
        return keep * got_a[slot] + (1.0 - keep), keep * got_s[slot]

    slot = 0
    decay = state = None
    for r, ks in enumerate(SCAN_ROUNDS):
        first = slot
        copies = []
        for k in ks:
            if r == 0:
                copies += send(slot, k, s_ref, a_ref)
            else:
                copies += send(slot, k, cur_s.at[r - 1], cur_a.at[r - 1])
            slot += 1
        for copy in copies:
            copy.wait()
        acc_a, acc_s = arrived(first + len(ks) - 1, ks[-1])
        for j in range(len(ks) - 2, -1, -1):
            part_a, part_s = arrived(first + j, ks[j])
            acc_s = part_a * acc_s + part_s
            acc_a = part_a * acc_a
        if r > 0:
            acc_s = cur_a[r - 1] * acc_s + cur_s[r - 1]
            acc_a = cur_a[r - 1] * acc_a
        if r + 1 < len(SCAN_ROUNDS):
            cur_s[r] = acc_s
            cur_a[r] = acc_a
        else:
            o_ref[...] = acc_s


def carry_scan(local_state, carry_decay):
    rounds = len(SCAN_ROUNDS) - 1
    slots = sum(len(ks) for ks in SCAN_ROUNDS)
    return pl.pallas_call(
        carry_scan_kernel,
        out_shape=jax.ShapeDtypeStruct(local_state.shape, local_state.dtype),
        in_specs=[pl.BlockSpec(memory_space=pltpu.VMEM)] * 2,
        out_specs=pl.BlockSpec(memory_space=pltpu.VMEM),
        scratch_shapes=[
            pltpu.VMEM((rounds,) + local_state.shape, jnp.float32),
            pltpu.VMEM((rounds,) + carry_decay.shape, jnp.float32),
            pltpu.VMEM((slots,) + local_state.shape, jnp.float32),
            pltpu.VMEM((slots,) + carry_decay.shape, jnp.float32),
            pltpu.SemaphoreType.DMA((2, 2, slots)),
        ],
        compiler_params=pltpu.CompilerParams(collective_id=0, has_side_effects=True),
    )(local_state, carry_decay)


def tp_sum_kernel(x_ref, o_ref, got, sems):
    n = lax.axis_size("tp")
    me = lax.axis_index("tp")
    row = lax.axis_index("ctx")
    barrier = pltpu.get_barrier_semaphore()
    for k in range(1, n):
        pl.semaphore_signal(
            barrier, inc=1, device_id=(row, lax.rem(me + k, n)), device_id_type=pl.DeviceIdType.MESH
        )
    pl.semaphore_wait(barrier, n - 1)
    copies = []
    for k in range(1, n):
        copy = pltpu.make_async_remote_copy(
            src_ref=x_ref,
            dst_ref=got.at[me],
            send_sem=sems.at[0, k],
            recv_sem=sems.at[1, k],
            device_id=(row, lax.rem(me + k, n)),
            device_id_type=pl.DeviceIdType.MESH,
        )
        copy.start()
        copies.append(copy)
    got[me] = x_ref[...]
    for k in range(1, n):
        copies[k - 1].wait_send()
        arriving = pltpu.make_async_remote_copy(
            src_ref=x_ref,
            dst_ref=got.at[lax.rem(me - k + n, n)],
            send_sem=sems.at[0, k],
            recv_sem=sems.at[1, k],
            device_id=(row, lax.rem(me + k, n)),
            device_id_type=pl.DeviceIdType.MESH,
        )
        arriving.wait_recv()
    total = got[0]
    for j in range(1, n):
        total = total + got[j]
    o_ref[...] = total


def tp_sum(values):
    n = lax.axis_size("tp")
    rows = values.size // 128
    shaped = jnp.pad(values.reshape(rows, 128), ((0, (-rows) % 8), (0, 0)))
    out = pl.pallas_call(
        tp_sum_kernel,
        out_shape=jax.ShapeDtypeStruct(shaped.shape, shaped.dtype),
        in_specs=[pl.BlockSpec(memory_space=pltpu.VMEM)],
        out_specs=pl.BlockSpec(memory_space=pltpu.VMEM),
        scratch_shapes=[
            pltpu.VMEM((n,) + shaped.shape, shaped.dtype),
            pltpu.SemaphoreType.DMA((2, n)),
        ],
        compiler_params=pltpu.CompilerParams(collective_id=1, has_side_effects=True),
    )(shaped)
    return out.reshape(-1)[: values.size]


def mamba_mix(ssm_input, gate, state_in, state_out, step_size, decay_log, skip_gain, norm_gain):
    careful = lax.Precision.HIGH
    row_count = ssm_input.shape[0]
    head_count = step_size.shape[1]
    inner_width = ssm_input.shape[1]
    inputs = ssm_input.astype(jnp.float32).reshape(row_count, head_count, SSM_HEAD_DIM)
    in_map = state_in.astype(jnp.float32)
    out_map = state_out.astype(jnp.float32)
    log_steps = -jnp.exp(decay_log)[None, :] * step_size
    cumulative = jnp.cumsum(log_steps, axis=0)
    grouped_per_head = cumulative.T
    lower = jnp.arange(row_count)[:, None] >= jnp.arange(row_count)[None, :]
    decay = jnp.where(
        lower[None],
        jnp.exp(jnp.minimum(grouped_per_head[:, :, None] - grouped_per_head[:, None, :], 0.0)),
        0.0,
    )
    inner = jnp.dot(state_out, state_in.T, preferred_element_type=jnp.float32)
    weighted = inputs * step_size[:, :, None]
    within = jnp.einsum("hts,shp->thp", decay * inner[None], weighted, precision=careful)
    tail = jnp.exp(cumulative[-1][None, :] - cumulative)
    local_state = jnp.einsum(
        "sn,shp->nhp", in_map, weighted * tail[:, :, None], precision=careful
    ).reshape(D_STATE, inner_width)
    carry_decay = jnp.repeat(jnp.exp(cumulative[-1]), SSM_HEAD_DIM)[None, :]

    incoming = carry_scan(local_state, carry_decay)

    from_past = jnp.dot(
        out_map, incoming, precision=careful, preferred_element_type=jnp.float32
    ).reshape(row_count, head_count, SSM_HEAD_DIM)
    from_past = from_past * jnp.exp(cumulative)[:, :, None]
    mixed = (within + from_past + skip_gain[None, :, None] * inputs).reshape(row_count, inner_width)
    gate_full = gate.astype(jnp.float32)
    gated = mixed * gate_full * jax.nn.sigmoid(gate_full)
    squares = tp_sum(jnp.sum(gated * gated, axis=1))
    scaled = gated * lax.rsqrt(squares / INNER + 1e-05)[:, None] * norm_gain[None, :]
    return scaled.astype(jnp.bfloat16)


def local(
    queries,
    keys,
    values,
    vertical,
    slash,
    block_position,
    ssm_input,
    gate,
    state_in,
    state_out,
    step_size,
    decay_log,
    skip_gain,
    norm_gain,
):
    kv_local = jnp.stack((keys, values))
    kv_local, ssm_input, step_size, decay_log, state_in = lax.optimization_barrier(
        (kv_local, ssm_input, step_size, decay_log, state_in)
    )
    attention_out = attend_sparse(queries, kv_local, vertical, slash, block_position)
    recurrent_mixer_result = mamba_mix(
        ssm_input, gate, state_in, state_out, step_size, decay_log, skip_gain, norm_gain
    )
    return (attention_out, recurrent_mixer_result)


def solution(mesh):
    return jax.shard_map(
        local,
        mesh=mesh,
        in_specs=(
            P("ctx", "tp"),
            P("ctx", "tp"),
            P("ctx", "tp"),
            P("tp", None),
            P("tp", None),
            P(),
            P("ctx", "tp"),
            P("ctx", "tp"),
            P("ctx", None),
            P("ctx", None),
            P("ctx", "tp"),
            P("tp"),
            P("tp"),
            P("tp"),
        ),
        out_specs=(P("ctx", "tp"), P("ctx", "tp")),
        check_vma=False,
    )
```

```python
import math

import jax
import jax.numpy as jnp
from jax import lax
from jax.experimental import pallas as pl
from jax.experimental.pallas import tpu as pltpu
from jax.sharding import PartitionSpec as P

HEAD_DIM = 128
SSM_HEAD_DIM = 64
D_STATE = 16
BLOCK = 64
INNER = 16384
NEG_FILL = -1e30


def shifted(array, axis, by):
    size = lax.axis_size(axis)
    pairs = [(i, i + by) for i in range(size) if 0 <= i + by < size]
    return lax.ppermute(array, axis, pairs)


def key_block_table(vertical, slash, block_position, blocks_here):
    my_index = lax.axis_index("ctx")
    total_blocks = block_position.shape[0]
    query_seq = lax.dynamic_slice_in_dim(block_position, my_index * blocks_here, blocks_here)
    heads = vertical.shape[0]
    br = query_seq[None, :, None]
    cand_v = jnp.broadcast_to(vertical[:, None, :], (heads, blocks_here, vertical.shape[1]))
    cand_s = br - slash[:, None, :]
    cand = jnp.concatenate([cand_v, cand_s], axis=-1)
    ok = jnp.concatenate([cand_v < br, cand_s >= 0], axis=-1)
    count = cand.shape[-1]
    earlier = jnp.arange(count)[None, :] < jnp.arange(count)[:, None]
    dup = jnp.any(
        (cand[..., :, None] == cand[..., None, :]) & ok[..., None, :] & earlier[None, None], axis=-1
    )
    ok = ok & ~dup
    diag = jnp.broadcast_to(query_seq[None, :, None], (heads, blocks_here, 1))
    cand = jnp.concatenate([diag, cand, jnp.zeros_like(diag)], axis=-1)
    ok = jnp.concatenate([jnp.ones_like(diag, bool), ok, jnp.zeros_like(diag, bool)], axis=-1)
    match = block_position[None, None, None, :] == cand[..., None]
    index = jnp.sum(jnp.where(match, jnp.arange(total_blocks, dtype=jnp.int32), 0), axis=-1)
    slots = cand.shape[-1]
    units = heads * blocks_here
    col_bias = jnp.where(ok.reshape(units, slots), 0.0, NEG_FILL).astype(jnp.float32)
    col_bias = jnp.repeat(col_bias, BLOCK, axis=-1)
    return index.reshape(units, slots).astype(jnp.int32), col_bias, slots


def sparse_attention_kernel(slots, blocks_here, q_ref, kv_ref, idx_ref, bias_ref, causal_ref, o_ref, kbuf, vbuf):
    score_scale = 1.0 / math.sqrt(HEAD_DIM)
    units = bias_ref.shape[0]

    def unit(i, carry):
        head = i // blocks_here
        qblock = i % blocks_here
        for j in range(slots):
            src = pl.multiple_of(idx_ref[i, j] * BLOCK, BLOCK)
            kbuf[pl.ds(j * BLOCK, BLOCK), :] = kv_ref[0, pl.ds(src, BLOCK), :]
            vbuf[pl.ds(j * BLOCK, BLOCK), :] = kv_ref[1, pl.ds(src, BLOCK), :]
        rows = pl.ds(pl.multiple_of(qblock * BLOCK, BLOCK), BLOCK)
        cols = pl.ds(pl.multiple_of(head * HEAD_DIM, HEAD_DIM), HEAD_DIM)
        q = q_ref[rows, cols]
        scores = lax.dot_general(
            q, kbuf[...], (((1,), (1,)), ((), ())), preferred_element_type=jnp.float32
        ) * score_scale
        masked = scores + causal_ref[...] + bias_ref[pl.ds(i, 1), :]
        top = jnp.max(masked, axis=1, keepdims=True)
        expo = jnp.exp(masked - top)
        denom = jnp.sum(expo, axis=1, keepdims=True)
        out = jnp.dot(expo.astype(jnp.bfloat16), vbuf[...], preferred_element_type=jnp.float32)
        o_ref[rows, cols] = (out / denom).astype(o_ref.dtype)
        return carry

    lax.fori_loop(0, units, unit, 0, unroll=units)


def attend_sparse(queries, kv_local, vertical, slash, block_position):
    row_count = queries.shape[0]
    blocks_here = row_count // BLOCK
    kv_all = lax.all_gather(kv_local, "ctx", axis=1, tiled=True)
    index, col_bias, slots = key_block_table(vertical, slash, block_position, blocks_here)
    units = col_bias.shape[0]
    r = lax.broadcasted_iota(jnp.int32, (BLOCK, slots * BLOCK), 0)
    c = lax.broadcasted_iota(jnp.int32, (BLOCK, slots * BLOCK), 1)
    causal_bias = jnp.where((c < BLOCK) & (c > r), NEG_FILL, 0.0).astype(jnp.float32)
    flops = units * 4 * BLOCK * slots * BLOCK * HEAD_DIM
    return pl.pallas_call(
        lambda *refs: sparse_attention_kernel(slots, blocks_here, *refs),
        out_shape=jax.ShapeDtypeStruct(queries.shape, queries.dtype),
        in_specs=[
            pl.BlockSpec(memory_space=pltpu.VMEM),
            pl.BlockSpec(memory_space=pltpu.VMEM),
            pl.BlockSpec(memory_space=pltpu.SMEM),
            pl.BlockSpec(memory_space=pltpu.VMEM),
            pl.BlockSpec(memory_space=pltpu.VMEM),
        ],
        out_specs=pl.BlockSpec(memory_space=pltpu.VMEM),
        scratch_shapes=[
            pltpu.VMEM((slots * BLOCK, HEAD_DIM), jnp.bfloat16),
            pltpu.VMEM((slots * BLOCK, HEAD_DIM), jnp.bfloat16),
        ],
        cost_estimate=pl.CostEstimate(
            flops=flops,
            transcendentals=units * BLOCK * slots * BLOCK,
            bytes_accessed=2 * queries.size * 2 + kv_all.size * 2,
        ),
    )(queries, kv_all, index, col_bias, causal_bias)


SCAN_SHIFTS = (2, 4, 8, 16)


def carry_scan_kernel(s_ref, a_ref, o_ref, cur_s, cur_a, got_s, got_a, sems):
    n = lax.axis_size("ctx")
    me = lax.axis_index("ctx")
    tp = lax.axis_index("tp")
    shifts = (1,) + SCAN_SHIFTS
    barrier = pltpu.get_barrier_semaphore()
    partners = sorted({k % n for k in shifts} | {(-k) % n for k in shifts})
    for k in partners:
        pl.semaphore_signal(
            barrier, inc=1, device_id=(lax.rem(me + k, n), tp), device_id_type=pl.DeviceIdType.MESH
        )
    pl.semaphore_wait(barrier, len(partners))

    def send(slot, k, src_s, src_a):
        target = (lax.rem(me + k, n), tp)
        copies = [
            pltpu.make_async_remote_copy(
                src_ref=src,
                dst_ref=dst.at[slot],
                send_sem=sems.at[part, 0, slot],
                recv_sem=sems.at[part, 1, slot],
                device_id=target,
                device_id_type=pl.DeviceIdType.MESH,
            )
            for part, (src, dst) in enumerate(((src_s, got_s), (src_a, got_a)))
        ]
        for copy in copies:
            copy.start()
        return copies

    def keep_of(k):
        return ((me - k + n) // n).astype(jnp.float32)

    first = send(0, 1, s_ref, a_ref) + send(1, 2, s_ref, a_ref)
    for copy in first:
        copy.wait()
    keep1, keep2 = keep_of(1), keep_of(2)
    a1, a2 = got_a[0], got_a[1]
    state = keep1 * (got_s[0] + a1 * (keep2 * got_s[1]))
    decay = (keep1 * a1 + (1.0 - keep1)) * (keep2 * a2 + (1.0 - keep2))
    for j, k in enumerate(SCAN_SHIFTS):
        cur_s[j] = state
        cur_a[j] = decay
        slot = j + 2
        for copy in send(slot, k, cur_s.at[j], cur_a.at[j]):
            copy.wait()
        keep = keep_of(k)
        state = cur_s[j] + cur_a[j] * (keep * got_s[slot])
        decay = cur_a[j] * (keep * got_a[slot] + (1.0 - keep))
    o_ref[...] = state


def carry_scan(local_state, carry_decay):
    rounds = len(SCAN_SHIFTS)
    slots = rounds + 2
    return pl.pallas_call(
        carry_scan_kernel,
        out_shape=jax.ShapeDtypeStruct(local_state.shape, local_state.dtype),
        in_specs=[pl.BlockSpec(memory_space=pltpu.VMEM)] * 2,
        out_specs=pl.BlockSpec(memory_space=pltpu.VMEM),
        scratch_shapes=[
            pltpu.VMEM((rounds,) + local_state.shape, jnp.float32),
            pltpu.VMEM((rounds,) + carry_decay.shape, jnp.float32),
            pltpu.VMEM((slots,) + local_state.shape, jnp.float32),
            pltpu.VMEM((slots,) + carry_decay.shape, jnp.float32),
            pltpu.SemaphoreType.DMA((2, 2, slots)),
        ],
        compiler_params=pltpu.CompilerParams(collective_id=0, has_side_effects=True),
    )(local_state, carry_decay)


def tp_sum_kernel(x_ref, o_ref, got, sems):
    n = lax.axis_size("tp")
    me = lax.axis_index("tp")
    row = lax.axis_index("ctx")
    barrier = pltpu.get_barrier_semaphore()
    for k in range(1, n):
        pl.semaphore_signal(
            barrier, inc=1, device_id=(row, lax.rem(me + k, n)), device_id_type=pl.DeviceIdType.MESH
        )
    pl.semaphore_wait(barrier, n - 1)
    copies = []
    for k in range(1, n):
        copy = pltpu.make_async_remote_copy(
            src_ref=x_ref,
            dst_ref=got.at[me],
            send_sem=sems.at[0, k],
            recv_sem=sems.at[1, k],
            device_id=(row, lax.rem(me + k, n)),
            device_id_type=pl.DeviceIdType.MESH,
        )
        copy.start()
        copies.append(copy)
    got[me] = x_ref[...]
    for k in range(1, n):
        copies[k - 1].wait_send()
        arriving = pltpu.make_async_remote_copy(
            src_ref=x_ref,
            dst_ref=got.at[lax.rem(me - k + n, n)],
            send_sem=sems.at[0, k],
            recv_sem=sems.at[1, k],
            device_id=(row, lax.rem(me + k, n)),
            device_id_type=pl.DeviceIdType.MESH,
        )
        arriving.wait_recv()
    total = got[0]
    for j in range(1, n):
        total = total + got[j]
    o_ref[...] = total


def tp_sum(values):
    n = lax.axis_size("tp")
    rows = values.size // 128
    shaped = jnp.pad(values.reshape(rows, 128), ((0, (-rows) % 8), (0, 0)))
    out = pl.pallas_call(
        tp_sum_kernel,
        out_shape=jax.ShapeDtypeStruct(shaped.shape, shaped.dtype),
        in_specs=[pl.BlockSpec(memory_space=pltpu.VMEM)],
        out_specs=pl.BlockSpec(memory_space=pltpu.VMEM),
        scratch_shapes=[
            pltpu.VMEM((n,) + shaped.shape, shaped.dtype),
            pltpu.SemaphoreType.DMA((2, n)),
        ],
        compiler_params=pltpu.CompilerParams(collective_id=1, has_side_effects=True),
    )(shaped)
    return out.reshape(-1)[: values.size]


def mamba_mix(ssm_input, gate, state_in, state_out, step_size, decay_log, skip_gain, norm_gain):
    careful = lax.Precision.HIGH
    row_count = ssm_input.shape[0]
    head_count = step_size.shape[1]
    inner_width = ssm_input.shape[1]
    inputs = ssm_input.astype(jnp.float32).reshape(row_count, head_count, SSM_HEAD_DIM)
    in_map = state_in.astype(jnp.float32)
    out_map = state_out.astype(jnp.float32)
    log_steps = -jnp.exp(decay_log)[None, :] * step_size
    cumulative = jnp.cumsum(log_steps, axis=0)
    grouped_per_head = cumulative.T
    lower = jnp.arange(row_count)[:, None] >= jnp.arange(row_count)[None, :]
    decay = jnp.where(
        lower[None],
        jnp.exp(jnp.minimum(grouped_per_head[:, :, None] - grouped_per_head[:, None, :], 0.0)),
        0.0,
    )
    inner = jnp.dot(state_out, state_in.T, preferred_element_type=jnp.float32)
    weighted = inputs * step_size[:, :, None]
    within = jnp.einsum("hts,shp->thp", decay * inner[None], weighted, precision=careful)
    tail = jnp.exp(cumulative[-1][None, :] - cumulative)
    local_state = jnp.einsum(
        "sn,shp->nhp", in_map, weighted * tail[:, :, None], precision=careful
    ).reshape(D_STATE, inner_width)
    carry_decay = jnp.repeat(jnp.exp(cumulative[-1]), SSM_HEAD_DIM)[None, :]

    incoming = carry_scan(local_state, carry_decay)

    from_past = jnp.dot(
        out_map, incoming, precision=careful, preferred_element_type=jnp.float32
    ).reshape(row_count, head_count, SSM_HEAD_DIM)
    from_past = from_past * jnp.exp(cumulative)[:, :, None]
    mixed = (within + from_past + skip_gain[None, :, None] * inputs).reshape(row_count, inner_width)
    gate_full = gate.astype(jnp.float32)
    gated = mixed * gate_full * jax.nn.sigmoid(gate_full)
    squares = tp_sum(jnp.sum(gated * gated, axis=1))
    scaled = gated * lax.rsqrt(squares / INNER + 1e-05)[:, None] * norm_gain[None, :]
    return scaled.astype(jnp.bfloat16)


def local(
    queries,
    keys,
    values,
    vertical,
    slash,
    block_position,
    ssm_input,
    gate,
    state_in,
    state_out,
    step_size,
    decay_log,
    skip_gain,
    norm_gain,
):
    kv_local = jnp.stack((keys, values))
    kv_local, ssm_input, step_size, decay_log, state_in = lax.optimization_barrier(
        (kv_local, ssm_input, step_size, decay_log, state_in)
    )
    attention_out = attend_sparse(queries, kv_local, vertical, slash, block_position)
    recurrent_mixer_result = mamba_mix(
        ssm_input, gate, state_in, state_out, step_size, decay_log, skip_gain, norm_gain
    )
    return (attention_out, recurrent_mixer_result)


def solution(mesh):
    return jax.shard_map(
        local,
        mesh=mesh,
        in_specs=(
            P("ctx", "tp"),
            P("ctx", "tp"),
            P("ctx", "tp"),
            P("tp", None),
            P("tp", None),
            P(),
            P("ctx", "tp"),
            P("ctx", "tp"),
            P("ctx", None),
            P("ctx", None),
            P("ctx", "tp"),
            P("tp"),
            P("tp"),
            P("tp"),
        ),
        out_specs=(P("ctx", "tp"), P("ctx", "tp")),
        check_vma=False,
    )
```

```python
import math

import jax
import jax.numpy as jnp
from jax import lax
from jax.experimental import pallas as pl
from jax.experimental.pallas import tpu as pltpu
from jax.sharding import PartitionSpec as P

HEAD_DIM = 128
SSM_HEAD_DIM = 64
D_STATE = 16
BLOCK = 64
INNER = 16384
NEG_FILL = -1e30


def shifted(array, axis, by):
    size = lax.axis_size(axis)
    pairs = [(i, i + by) for i in range(size) if 0 <= i + by < size]
    return lax.ppermute(array, axis, pairs)


def key_block_table(vertical, slash, block_position, blocks_here):
    my_index = lax.axis_index("ctx")
    total_blocks = block_position.shape[0]
    query_seq = lax.dynamic_slice_in_dim(block_position, my_index * blocks_here, blocks_here)
    heads = vertical.shape[0]
    br = query_seq[None, :, None]
    cand_v = jnp.broadcast_to(vertical[:, None, :], (heads, blocks_here, vertical.shape[1]))
    cand_s = br - slash[:, None, :]
    cand = jnp.concatenate([cand_v, cand_s], axis=-1)
    ok = jnp.concatenate([cand_v < br, cand_s >= 0], axis=-1)
    count = cand.shape[-1]
    earlier = jnp.arange(count)[None, :] < jnp.arange(count)[:, None]
    dup = jnp.any(
        (cand[..., :, None] == cand[..., None, :]) & ok[..., None, :] & earlier[None, None], axis=-1
    )
    ok = ok & ~dup
    diag = jnp.broadcast_to(query_seq[None, :, None], (heads, blocks_here, 1))
    cand = jnp.concatenate([diag, cand, jnp.zeros_like(diag)], axis=-1)
    ok = jnp.concatenate([jnp.ones_like(diag, bool), ok, jnp.zeros_like(diag, bool)], axis=-1)
    match = block_position[None, None, None, :] == cand[..., None]
    index = jnp.sum(jnp.where(match, jnp.arange(total_blocks, dtype=jnp.int32), 0), axis=-1)
    slots = cand.shape[-1]
    units = heads * blocks_here
    col_bias = jnp.where(ok.reshape(units, slots), 0.0, NEG_FILL).astype(jnp.float32)
    col_bias = jnp.repeat(col_bias, BLOCK, axis=-1)
    return index.reshape(units, slots).astype(jnp.int32), col_bias, slots


def sparse_attention_kernel(slots, blocks_here, q_ref, kv_ref, idx_ref, bias_ref, causal_ref, o_ref, kbuf, vbuf):
    score_scale = 1.0 / math.sqrt(HEAD_DIM)
    units = bias_ref.shape[0]

    def unit(i, carry):
        head = i // blocks_here
        qblock = i % blocks_here
        for j in range(slots):
            src = pl.multiple_of(idx_ref[i, j] * BLOCK, BLOCK)
            kbuf[pl.ds(j * BLOCK, BLOCK), :] = kv_ref[0, pl.ds(src, BLOCK), :]
            vbuf[pl.ds(j * BLOCK, BLOCK), :] = kv_ref[1, pl.ds(src, BLOCK), :]
        rows = pl.ds(pl.multiple_of(qblock * BLOCK, BLOCK), BLOCK)
        cols = pl.ds(pl.multiple_of(head * HEAD_DIM, HEAD_DIM), HEAD_DIM)
        q = q_ref[rows, cols]
        scores = lax.dot_general(
            q, kbuf[...], (((1,), (1,)), ((), ())), preferred_element_type=jnp.float32
        ) * score_scale
        masked = scores + causal_ref[...] + bias_ref[pl.ds(i, 1), :]
        top = jnp.max(masked, axis=1, keepdims=True)
        expo = jnp.exp(masked - top)
        denom = jnp.sum(expo, axis=1, keepdims=True)
        out = jnp.dot(expo.astype(jnp.bfloat16), vbuf[...], preferred_element_type=jnp.float32)
        o_ref[rows, cols] = (out / denom).astype(o_ref.dtype)
        return carry

    lax.fori_loop(0, units, unit, 0, unroll=units)


def attend_sparse(queries, kv_local, vertical, slash, block_position):
    row_count = queries.shape[0]
    blocks_here = row_count // BLOCK
    kv_all = lax.all_gather(kv_local, "ctx", axis=1, tiled=True)
    index, col_bias, slots = key_block_table(vertical, slash, block_position, blocks_here)
    units = col_bias.shape[0]
    r = lax.broadcasted_iota(jnp.int32, (BLOCK, slots * BLOCK), 0)
    c = lax.broadcasted_iota(jnp.int32, (BLOCK, slots * BLOCK), 1)
    causal_bias = jnp.where((c < BLOCK) & (c > r), NEG_FILL, 0.0).astype(jnp.float32)
    flops = units * 4 * BLOCK * slots * BLOCK * HEAD_DIM
    return pl.pallas_call(
        lambda *refs: sparse_attention_kernel(slots, blocks_here, *refs),
        out_shape=jax.ShapeDtypeStruct(queries.shape, queries.dtype),
        in_specs=[
            pl.BlockSpec(memory_space=pltpu.VMEM),
            pl.BlockSpec(memory_space=pltpu.VMEM),
            pl.BlockSpec(memory_space=pltpu.SMEM),
            pl.BlockSpec(memory_space=pltpu.VMEM),
            pl.BlockSpec(memory_space=pltpu.VMEM),
        ],
        out_specs=pl.BlockSpec(memory_space=pltpu.VMEM),
        scratch_shapes=[
            pltpu.VMEM((slots * BLOCK, HEAD_DIM), jnp.bfloat16),
            pltpu.VMEM((slots * BLOCK, HEAD_DIM), jnp.bfloat16),
        ],
        cost_estimate=pl.CostEstimate(
            flops=flops,
            transcendentals=units * BLOCK * slots * BLOCK,
            bytes_accessed=2 * queries.size * 2 + kv_all.size * 2,
        ),
    )(queries, kv_all, index, col_bias, causal_bias)


SCAN_SHIFTS = (2, 4, 8, 16)


def carry_scan_kernel(x_ref, o_ref, cur, got, sems):
    n = lax.axis_size("ctx")
    me = lax.axis_index("ctx")
    tp = lax.axis_index("tp")
    rows = D_STATE
    shifts = (1,) + SCAN_SHIFTS
    barrier = pltpu.get_barrier_semaphore()
    partners = sorted({k % n for k in shifts} | {(-k) % n for k in shifts})
    for k in partners:
        pl.semaphore_signal(
            barrier, inc=1, device_id=(lax.rem(me + k, n), tp), device_id_type=pl.DeviceIdType.MESH
        )
    pl.semaphore_wait(barrier, len(partners))

    def send(slot, k, src):
        copy = pltpu.make_async_remote_copy(
            src_ref=src,
            dst_ref=got.at[slot],
            send_sem=sems.at[0, slot],
            recv_sem=sems.at[1, slot],
            device_id=(lax.rem(me + k, n), tp),
            device_id_type=pl.DeviceIdType.MESH,
        )
        copy.start()
        return copy

    def keep_of(k):
        return ((me - k + n) // n).astype(jnp.float32)

    first = [send(0, 1, x_ref), send(1, 2, x_ref)]
    for copy in first:
        copy.wait()
    keep1, keep2 = keep_of(1), keep_of(2)
    g0, g1 = got[0], got[1]
    a1, a2 = g0[rows:], g1[rows:]
    state = keep1 * (g0[:rows] + a1 * (keep2 * g1[:rows]))
    decay = (keep1 * a1 + (1.0 - keep1)) * (keep2 * a2 + (1.0 - keep2))
    for j, k in enumerate(SCAN_SHIFTS):
        cur[j] = jnp.concatenate([state, decay], axis=0)
        slot = j + 2
        send(slot, k, cur.at[j]).wait()
        keep = keep_of(k)
        mine, arrived = cur[j], got[slot]
        state = mine[:rows] + mine[rows:] * (keep * arrived[:rows])
        decay = mine[rows:] * (keep * arrived[rows:] + (1.0 - keep))
    o_ref[...] = state


def carry_scan(local_state, carry_decay):
    rounds = len(SCAN_SHIFTS)
    slots = rounds + 2
    packed = jnp.concatenate([local_state, carry_decay], axis=0)
    return pl.pallas_call(
        carry_scan_kernel,
        out_shape=jax.ShapeDtypeStruct(local_state.shape, local_state.dtype),
        in_specs=[pl.BlockSpec(memory_space=pltpu.VMEM)],
        out_specs=pl.BlockSpec(memory_space=pltpu.VMEM),
        scratch_shapes=[
            pltpu.VMEM((rounds,) + packed.shape, jnp.float32),
            pltpu.VMEM((slots,) + packed.shape, jnp.float32),
            pltpu.SemaphoreType.DMA((2, slots)),
        ],
        compiler_params=pltpu.CompilerParams(collective_id=0, has_side_effects=True),
    )(packed)


def tp_sum_kernel(x_ref, o_ref, got, sems):
    n = lax.axis_size("tp")
    me = lax.axis_index("tp")
    row = lax.axis_index("ctx")
    barrier = pltpu.get_barrier_semaphore()
    for k in range(1, n):
        pl.semaphore_signal(
            barrier, inc=1, device_id=(row, lax.rem(me + k, n)), device_id_type=pl.DeviceIdType.MESH
        )
    pl.semaphore_wait(barrier, n - 1)
    copies = []
    for k in range(1, n):
        copy = pltpu.make_async_remote_copy(
            src_ref=x_ref,
            dst_ref=got.at[me],
            send_sem=sems.at[0, k],
            recv_sem=sems.at[1, k],
            device_id=(row, lax.rem(me + k, n)),
            device_id_type=pl.DeviceIdType.MESH,
        )
        copy.start()
        copies.append(copy)
    got[me] = x_ref[...]
    for k in range(1, n):
        copies[k - 1].wait_send()
        arriving = pltpu.make_async_remote_copy(
            src_ref=x_ref,
            dst_ref=got.at[lax.rem(me - k + n, n)],
            send_sem=sems.at[0, k],
            recv_sem=sems.at[1, k],
            device_id=(row, lax.rem(me + k, n)),
            device_id_type=pl.DeviceIdType.MESH,
        )
        arriving.wait_recv()
    total = got[0]
    for j in range(1, n):
        total = total + got[j]
    o_ref[...] = total


def tp_sum(values):
    n = lax.axis_size("tp")
    rows = values.size // 128
    shaped = jnp.pad(values.reshape(rows, 128), ((0, (-rows) % 8), (0, 0)))
    out = pl.pallas_call(
        tp_sum_kernel,
        out_shape=jax.ShapeDtypeStruct(shaped.shape, shaped.dtype),
        in_specs=[pl.BlockSpec(memory_space=pltpu.VMEM)],
        out_specs=pl.BlockSpec(memory_space=pltpu.VMEM),
        scratch_shapes=[
            pltpu.VMEM((n,) + shaped.shape, shaped.dtype),
            pltpu.SemaphoreType.DMA((2, n)),
        ],
        compiler_params=pltpu.CompilerParams(collective_id=1, has_side_effects=True),
    )(shaped)
    return out.reshape(-1)[: values.size]


def mamba_mix(ssm_input, gate, state_in, state_out, step_size, decay_log, skip_gain, norm_gain):
    careful = lax.Precision.HIGH
    row_count = ssm_input.shape[0]
    head_count = step_size.shape[1]
    inner_width = ssm_input.shape[1]
    inputs = ssm_input.astype(jnp.float32).reshape(row_count, head_count, SSM_HEAD_DIM)
    in_map = state_in.astype(jnp.float32)
    out_map = state_out.astype(jnp.float32)
    log_steps = -jnp.exp(decay_log)[None, :] * step_size
    cumulative = jnp.cumsum(log_steps, axis=0)
    grouped_per_head = cumulative.T
    lower = jnp.arange(row_count)[:, None] >= jnp.arange(row_count)[None, :]
    decay = jnp.where(
        lower[None],
        jnp.exp(jnp.minimum(grouped_per_head[:, :, None] - grouped_per_head[:, None, :], 0.0)),
        0.0,
    )
    inner = jnp.dot(state_out, state_in.T, preferred_element_type=jnp.float32)
    weighted = inputs * step_size[:, :, None]
    within = jnp.einsum("hts,shp->thp", decay * inner[None], weighted, precision=careful)
    tail = jnp.exp(cumulative[-1][None, :] - cumulative)
    local_state = jnp.einsum(
        "sn,shp->nhp", in_map, weighted * tail[:, :, None], precision=careful
    ).reshape(D_STATE, inner_width)
    carry_decay = jnp.repeat(jnp.exp(cumulative[-1]), SSM_HEAD_DIM)[None, :]

    incoming = carry_scan(local_state, carry_decay)

    from_past = jnp.dot(
        out_map, incoming, precision=careful, preferred_element_type=jnp.float32
    ).reshape(row_count, head_count, SSM_HEAD_DIM)
    from_past = from_past * jnp.exp(cumulative)[:, :, None]
    mixed = (within + from_past + skip_gain[None, :, None] * inputs).reshape(row_count, inner_width)
    gate_full = gate.astype(jnp.float32)
    gated = mixed * gate_full * jax.nn.sigmoid(gate_full)
    squares = tp_sum(jnp.sum(gated * gated, axis=1))
    scaled = gated * lax.rsqrt(squares / INNER + 1e-05)[:, None] * norm_gain[None, :]
    return scaled.astype(jnp.bfloat16)


def local(
    queries,
    keys,
    values,
    vertical,
    slash,
    block_position,
    ssm_input,
    gate,
    state_in,
    state_out,
    step_size,
    decay_log,
    skip_gain,
    norm_gain,
):
    kv_local = jnp.stack((keys, values))
    kv_local, ssm_input, step_size, decay_log, state_in = lax.optimization_barrier(
        (kv_local, ssm_input, step_size, decay_log, state_in)
    )
    attention_out = attend_sparse(queries, kv_local, vertical, slash, block_position)
    recurrent_mixer_result = mamba_mix(
        ssm_input, gate, state_in, state_out, step_size, decay_log, skip_gain, norm_gain
    )
    return (attention_out, recurrent_mixer_result)


def solution(mesh):
    return jax.shard_map(
        local,
        mesh=mesh,
        in_specs=(
            P("ctx", "tp"),
            P("ctx", "tp"),
            P("ctx", "tp"),
            P("tp", None),
            P("tp", None),
            P(),
            P("ctx", "tp"),
            P("ctx", "tp"),
            P("ctx", None),
            P("ctx", None),
            P("ctx", "tp"),
            P("tp"),
            P("tp"),
            P("tp"),
        ),
        out_specs=(P("ctx", "tp"), P("ctx", "tp")),
        check_vma=False,
    )
```

```python
import math

import jax
import jax.numpy as jnp
from jax import lax
from jax.experimental import pallas as pl
from jax.experimental.pallas import tpu as pltpu
from jax.sharding import PartitionSpec as P

HEAD_DIM = 128
SSM_HEAD_DIM = 64
D_STATE = 16
BLOCK = 64
INNER = 16384
NEG_FILL = -1e30


def shifted(array, axis, by):
    size = lax.axis_size(axis)
    pairs = [(i, i + by) for i in range(size) if 0 <= i + by < size]
    return lax.ppermute(array, axis, pairs)


def key_block_table(vertical, slash, block_position, blocks_here):
    my_index = lax.axis_index("ctx")
    total_blocks = block_position.shape[0]
    query_seq = lax.dynamic_slice_in_dim(block_position, my_index * blocks_here, blocks_here)
    heads = vertical.shape[0]
    br = query_seq[None, :, None]
    cand_v = jnp.broadcast_to(vertical[:, None, :], (heads, blocks_here, vertical.shape[1]))
    cand_s = br - slash[:, None, :]
    cand = jnp.concatenate([cand_v, cand_s], axis=-1)
    ok = jnp.concatenate([cand_v < br, cand_s >= 0], axis=-1)
    count = cand.shape[-1]
    earlier = jnp.arange(count)[None, :] < jnp.arange(count)[:, None]
    dup = jnp.any(
        (cand[..., :, None] == cand[..., None, :]) & ok[..., None, :] & earlier[None, None], axis=-1
    )
    ok = ok & ~dup
    diag = jnp.broadcast_to(query_seq[None, :, None], (heads, blocks_here, 1))
    cand = jnp.concatenate([diag, cand, jnp.zeros_like(diag)], axis=-1)
    ok = jnp.concatenate([jnp.ones_like(diag, bool), ok, jnp.zeros_like(diag, bool)], axis=-1)
    match = block_position[None, None, None, :] == cand[..., None]
    index = jnp.sum(jnp.where(match, jnp.arange(total_blocks, dtype=jnp.int32), 0), axis=-1)
    slots = cand.shape[-1]
    units = heads * blocks_here
    col_bias = jnp.where(ok.reshape(units, slots), 0.0, NEG_FILL).astype(jnp.float32)
    col_bias = jnp.repeat(col_bias, BLOCK, axis=-1)
    return index.reshape(units, slots).astype(jnp.int32), col_bias, slots


def sparse_attention_kernel(slots, blocks_here, q_ref, kv_ref, idx_ref, bias_ref, causal_ref, o_ref, kbuf, vbuf):
    score_scale = 1.0 / math.sqrt(HEAD_DIM)
    units = bias_ref.shape[0]

    def unit(i, carry):
        head = i // blocks_here
        qblock = i % blocks_here
        for j in range(slots):
            src = pl.multiple_of(idx_ref[i, j] * BLOCK, BLOCK)
            kbuf[pl.ds(j * BLOCK, BLOCK), :] = kv_ref[0, pl.ds(src, BLOCK), :]
            vbuf[pl.ds(j * BLOCK, BLOCK), :] = kv_ref[1, pl.ds(src, BLOCK), :]
        rows = pl.ds(pl.multiple_of(qblock * BLOCK, BLOCK), BLOCK)
        cols = pl.ds(pl.multiple_of(head * HEAD_DIM, HEAD_DIM), HEAD_DIM)
        q = q_ref[rows, cols]
        scores = lax.dot_general(
            q, kbuf[...], (((1,), (1,)), ((), ())), preferred_element_type=jnp.float32
        ) * score_scale
        masked = scores + causal_ref[...] + bias_ref[pl.ds(i, 1), :]
        top = jnp.max(masked, axis=1, keepdims=True)
        expo = jnp.exp(masked - top)
        denom = jnp.sum(expo, axis=1, keepdims=True)
        out = jnp.dot(expo.astype(jnp.bfloat16), vbuf[...], preferred_element_type=jnp.float32)
        o_ref[rows, cols] = (out / denom).astype(o_ref.dtype)
        return carry

    lax.fori_loop(0, units, unit, 0, unroll=units)


def attend_sparse(queries, kv_local, vertical, slash, block_position):
    row_count = queries.shape[0]
    blocks_here = row_count // BLOCK
    kv_all = lax.all_gather(kv_local, "ctx", axis=1, tiled=True)
    index, col_bias, slots = key_block_table(vertical, slash, block_position, blocks_here)
    units = col_bias.shape[0]
    r = lax.broadcasted_iota(jnp.int32, (BLOCK, slots * BLOCK), 0)
    c = lax.broadcasted_iota(jnp.int32, (BLOCK, slots * BLOCK), 1)
    causal_bias = jnp.where((c < BLOCK) & (c > r), NEG_FILL, 0.0).astype(jnp.float32)
    flops = units * 4 * BLOCK * slots * BLOCK * HEAD_DIM
    return pl.pallas_call(
        lambda *refs: sparse_attention_kernel(slots, blocks_here, *refs),
        out_shape=jax.ShapeDtypeStruct(queries.shape, queries.dtype),
        in_specs=[
            pl.BlockSpec(memory_space=pltpu.VMEM),
            pl.BlockSpec(memory_space=pltpu.VMEM),
            pl.BlockSpec(memory_space=pltpu.SMEM),
            pl.BlockSpec(memory_space=pltpu.VMEM),
            pl.BlockSpec(memory_space=pltpu.VMEM),
        ],
        out_specs=pl.BlockSpec(memory_space=pltpu.VMEM),
        scratch_shapes=[
            pltpu.VMEM((slots * BLOCK, HEAD_DIM), jnp.bfloat16),
            pltpu.VMEM((slots * BLOCK, HEAD_DIM), jnp.bfloat16),
        ],
        cost_estimate=pl.CostEstimate(
            flops=flops,
            transcendentals=units * BLOCK * slots * BLOCK,
            bytes_accessed=2 * queries.size * 2 + kv_all.size * 2,
        ),
    )(queries, kv_all, index, col_bias, causal_bias)


SCAN_SHIFTS = (2, 4, 8, 16)


def carry_scan_kernel(s_ref, a_ref, o_ref, cur_s, cur_a, got_s, got_a, sems):
    n = lax.axis_size("ctx")
    me = lax.axis_index("ctx")
    tp = lax.axis_index("tp")
    shifts = (1,) + SCAN_SHIFTS
    barrier = pltpu.get_barrier_semaphore()
    partners = sorted({k % n for k in shifts} | {(-k) % n for k in shifts})
    for k in partners:
        pl.semaphore_signal(
            barrier, inc=1, device_id=(lax.rem(me + k, n), tp), device_id_type=pl.DeviceIdType.MESH
        )
    pl.semaphore_wait(barrier, len(partners))

    def send(slot, k, src_s, src_a):
        target = (lax.rem(me + k, n), tp)
        half = src_s.shape[0] // 2
        pieces = (
            (src_s.at[pl.ds(0, half)], got_s.at[slot, pl.ds(0, half)]),
            (src_s.at[pl.ds(half, half)], got_s.at[slot, pl.ds(half, half)]),
            (src_a, got_a.at[slot]),
        )
        copies = [
            pltpu.make_async_remote_copy(
                src_ref=src,
                dst_ref=dst,
                send_sem=sems.at[part, 0, slot],
                recv_sem=sems.at[part, 1, slot],
                device_id=target,
                device_id_type=pl.DeviceIdType.MESH,
            )
            for part, (src, dst) in enumerate(pieces)
        ]
        for copy in copies:
            copy.start()
        return copies

    def keep_of(k):
        return ((me - k + n) // n).astype(jnp.float32)

    first = send(0, 1, s_ref, a_ref) + send(1, 2, s_ref, a_ref)
    for copy in first:
        copy.wait()
    keep1, keep2 = keep_of(1), keep_of(2)
    a1, a2 = got_a[0], got_a[1]
    state = keep1 * (got_s[0] + a1 * (keep2 * got_s[1]))
    decay = (keep1 * a1 + (1.0 - keep1)) * (keep2 * a2 + (1.0 - keep2))
    for j, k in enumerate(SCAN_SHIFTS):
        cur_s[j] = state
        cur_a[j] = decay
        slot = j + 2
        for copy in send(slot, k, cur_s.at[j], cur_a.at[j]):
            copy.wait()
        keep = keep_of(k)
        state = cur_s[j] + cur_a[j] * (keep * got_s[slot])
        decay = cur_a[j] * (keep * got_a[slot] + (1.0 - keep))
    o_ref[...] = state


def carry_scan(local_state, carry_decay):
    rounds = len(SCAN_SHIFTS)
    slots = rounds + 2
    return pl.pallas_call(
        carry_scan_kernel,
        out_shape=jax.ShapeDtypeStruct(local_state.shape, local_state.dtype),
        in_specs=[pl.BlockSpec(memory_space=pltpu.VMEM)] * 2,
        out_specs=pl.BlockSpec(memory_space=pltpu.VMEM),
        scratch_shapes=[
            pltpu.VMEM((rounds,) + local_state.shape, jnp.float32),
            pltpu.VMEM((rounds,) + carry_decay.shape, jnp.float32),
            pltpu.VMEM((slots,) + local_state.shape, jnp.float32),
            pltpu.VMEM((slots,) + carry_decay.shape, jnp.float32),
            pltpu.SemaphoreType.DMA((3, 2, slots)),
        ],
        compiler_params=pltpu.CompilerParams(collective_id=0, has_side_effects=True),
    )(local_state, carry_decay)


def tp_sum_kernel(x_ref, o_ref, got, sems):
    n = lax.axis_size("tp")
    me = lax.axis_index("tp")
    row = lax.axis_index("ctx")
    barrier = pltpu.get_barrier_semaphore()
    for k in range(1, n):
        pl.semaphore_signal(
            barrier, inc=1, device_id=(row, lax.rem(me + k, n)), device_id_type=pl.DeviceIdType.MESH
        )
    pl.semaphore_wait(barrier, n - 1)
    copies = []
    for k in range(1, n):
        copy = pltpu.make_async_remote_copy(
            src_ref=x_ref,
            dst_ref=got.at[me],
            send_sem=sems.at[0, k],
            recv_sem=sems.at[1, k],
            device_id=(row, lax.rem(me + k, n)),
            device_id_type=pl.DeviceIdType.MESH,
        )
        copy.start()
        copies.append(copy)
    got[me] = x_ref[...]
    for k in range(1, n):
        copies[k - 1].wait_send()
        arriving = pltpu.make_async_remote_copy(
            src_ref=x_ref,
            dst_ref=got.at[lax.rem(me - k + n, n)],
            send_sem=sems.at[0, k],
            recv_sem=sems.at[1, k],
            device_id=(row, lax.rem(me + k, n)),
            device_id_type=pl.DeviceIdType.MESH,
        )
        arriving.wait_recv()
    total = got[0]
    for j in range(1, n):
        total = total + got[j]
    o_ref[...] = total


def tp_sum(values):
    n = lax.axis_size("tp")
    rows = values.size // 128
    shaped = jnp.pad(values.reshape(rows, 128), ((0, (-rows) % 8), (0, 0)))
    out = pl.pallas_call(
        tp_sum_kernel,
        out_shape=jax.ShapeDtypeStruct(shaped.shape, shaped.dtype),
        in_specs=[pl.BlockSpec(memory_space=pltpu.VMEM)],
        out_specs=pl.BlockSpec(memory_space=pltpu.VMEM),
        scratch_shapes=[
            pltpu.VMEM((n,) + shaped.shape, shaped.dtype),
            pltpu.SemaphoreType.DMA((2, n)),
        ],
        compiler_params=pltpu.CompilerParams(collective_id=1, has_side_effects=True),
    )(shaped)
    return out.reshape(-1)[: values.size]


def mamba_mix(ssm_input, gate, state_in, state_out, step_size, decay_log, skip_gain, norm_gain):
    careful = lax.Precision.HIGH
    row_count = ssm_input.shape[0]
    head_count = step_size.shape[1]
    inner_width = ssm_input.shape[1]
    inputs = ssm_input.astype(jnp.float32).reshape(row_count, head_count, SSM_HEAD_DIM)
    in_map = state_in.astype(jnp.float32)
    out_map = state_out.astype(jnp.float32)
    log_steps = -jnp.exp(decay_log)[None, :] * step_size
    cumulative = jnp.cumsum(log_steps, axis=0)
    grouped_per_head = cumulative.T
    lower = jnp.arange(row_count)[:, None] >= jnp.arange(row_count)[None, :]
    decay = jnp.where(
        lower[None],
        jnp.exp(jnp.minimum(grouped_per_head[:, :, None] - grouped_per_head[:, None, :], 0.0)),
        0.0,
    )
    inner = jnp.dot(state_out, state_in.T, preferred_element_type=jnp.float32)
    weighted = inputs * step_size[:, :, None]
    within = jnp.einsum("hts,shp->thp", decay * inner[None], weighted, precision=careful)
    tail = jnp.exp(cumulative[-1][None, :] - cumulative)
    local_state = jnp.einsum(
        "sn,shp->nhp", in_map, weighted * tail[:, :, None], precision=careful
    ).reshape(D_STATE, inner_width)
    carry_decay = jnp.repeat(jnp.exp(cumulative[-1]), SSM_HEAD_DIM)[None, :]

    incoming = carry_scan(local_state, carry_decay)

    from_past = jnp.dot(
        out_map, incoming, precision=careful, preferred_element_type=jnp.float32
    ).reshape(row_count, head_count, SSM_HEAD_DIM)
    from_past = from_past * jnp.exp(cumulative)[:, :, None]
    mixed = (within + from_past + skip_gain[None, :, None] * inputs).reshape(row_count, inner_width)
    gate_full = gate.astype(jnp.float32)
    gated = mixed * gate_full * jax.nn.sigmoid(gate_full)
    squares = tp_sum(jnp.sum(gated * gated, axis=1))
    scaled = gated * lax.rsqrt(squares / INNER + 1e-05)[:, None] * norm_gain[None, :]
    return scaled.astype(jnp.bfloat16)


def local(
    queries,
    keys,
    values,
    vertical,
    slash,
    block_position,
    ssm_input,
    gate,
    state_in,
    state_out,
    step_size,
    decay_log,
    skip_gain,
    norm_gain,
):
    kv_local = jnp.stack((keys, values))
    kv_local, ssm_input, step_size, decay_log, state_in = lax.optimization_barrier(
        (kv_local, ssm_input, step_size, decay_log, state_in)
    )
    attention_out = attend_sparse(queries, kv_local, vertical, slash, block_position)
    recurrent_mixer_result = mamba_mix(
        ssm_input, gate, state_in, state_out, step_size, decay_log, skip_gain, norm_gain
    )
    return (attention_out, recurrent_mixer_result)


def solution(mesh):
    return jax.shard_map(
        local,
        mesh=mesh,
        in_specs=(
            P("ctx", "tp"),
            P("ctx", "tp"),
            P("ctx", "tp"),
            P("tp", None),
            P("tp", None),
            P(),
            P("ctx", "tp"),
            P("ctx", "tp"),
            P("ctx", None),
            P("ctx", None),
            P("ctx", "tp"),
            P("tp"),
            P("tp"),
            P("tp"),
        ),
        out_specs=(P("ctx", "tp"), P("ctx", "tp")),
        check_vma=False,
    )
```

```python
import math

import jax
import numpy as np
import jax.numpy as jnp
from jax import lax
from jax.experimental import pallas as pl
from jax.experimental.pallas import tpu as pltpu
from jax.sharding import PartitionSpec as P

HEAD_DIM = 128
SSM_HEAD_DIM = 64
D_STATE = 16
BLOCK = 64
INNER = 16384
NEG_FILL = -1e30


def shifted(array, axis, by):
    size = lax.axis_size(axis)
    pairs = [(i, i + by) for i in range(size) if 0 <= i + by < size]
    return lax.ppermute(array, axis, pairs)


def key_block_table(vertical, slash, block_position, blocks_here):
    my_index = lax.axis_index("ctx")
    total_blocks = block_position.shape[0]
    query_seq = lax.dynamic_slice_in_dim(block_position, my_index * blocks_here, blocks_here)
    heads = vertical.shape[0]
    br = query_seq[None, :, None]
    cand_v = jnp.broadcast_to(vertical[:, None, :], (heads, blocks_here, vertical.shape[1]))
    cand_s = br - slash[:, None, :]
    cand = jnp.concatenate([cand_v, cand_s], axis=-1)
    ok = jnp.concatenate([cand_v < br, cand_s >= 0], axis=-1)
    count = cand.shape[-1]
    earlier = jnp.arange(count)[None, :] < jnp.arange(count)[:, None]
    dup = jnp.any(
        (cand[..., :, None] == cand[..., None, :]) & ok[..., None, :] & earlier[None, None], axis=-1
    )
    ok = ok & ~dup
    diag = jnp.broadcast_to(query_seq[None, :, None], (heads, blocks_here, 1))
    cand = jnp.concatenate([diag, cand, jnp.zeros_like(diag)], axis=-1)
    ok = jnp.concatenate([jnp.ones_like(diag, bool), ok, jnp.zeros_like(diag, bool)], axis=-1)
    match = block_position[None, None, None, :] == cand[..., None]
    index = jnp.sum(jnp.where(match, jnp.arange(total_blocks, dtype=jnp.int32), 0), axis=-1)
    slots = cand.shape[-1]
    units = heads * blocks_here
    col_bias = jnp.where(ok.reshape(units, slots), 0.0, NEG_FILL).astype(jnp.float32)
    col_bias = jnp.repeat(col_bias, BLOCK, axis=-1)
    return index.reshape(units, slots).astype(jnp.int32), col_bias, slots


def sparse_attention_kernel(slots, blocks_here, q_ref, kv_ref, idx_ref, bias_ref, causal_ref, o_ref, kbuf, vbuf):
    score_scale = 1.0 / math.sqrt(HEAD_DIM)
    units = bias_ref.shape[0]

    def unit(i, carry):
        head = i // blocks_here
        qblock = i % blocks_here
        for j in range(slots):
            src = pl.multiple_of(idx_ref[i, j] * BLOCK, BLOCK)
            kbuf[pl.ds(j * BLOCK, BLOCK), :] = kv_ref[0, pl.ds(src, BLOCK), :]
            vbuf[pl.ds(j * BLOCK, BLOCK), :] = kv_ref[1, pl.ds(src, BLOCK), :]
        rows = pl.ds(pl.multiple_of(qblock * BLOCK, BLOCK), BLOCK)
        cols = pl.ds(pl.multiple_of(head * HEAD_DIM, HEAD_DIM), HEAD_DIM)
        q = q_ref[rows, cols]
        scores = lax.dot_general(
            q, kbuf[...], (((1,), (1,)), ((), ())), preferred_element_type=jnp.float32
        ) * score_scale
        masked = scores + causal_ref[...] + bias_ref[pl.ds(i, 1), :]
        top = jnp.max(masked, axis=1, keepdims=True)
        expo = jnp.exp(masked - top)
        denom = jnp.sum(expo, axis=1, keepdims=True)
        out = jnp.dot(expo.astype(jnp.bfloat16), vbuf[...], preferred_element_type=jnp.float32)
        o_ref[rows, cols] = (out / denom).astype(o_ref.dtype)
        return carry

    lax.fori_loop(0, units, unit, 0, unroll=units)


def attend_sparse(queries, kv_local, vertical, slash, block_position):
    row_count = queries.shape[0]
    blocks_here = row_count // BLOCK
    kv_all = lax.all_gather(kv_local, "ctx", axis=1, tiled=True)
    index, col_bias, slots = key_block_table(vertical, slash, block_position, blocks_here)
    units = col_bias.shape[0]
    r = np.arange(BLOCK)[:, None]
    c = np.arange(slots * BLOCK)[None, :]
    causal_bias = jnp.asarray(np.where((c < BLOCK) & (c > r), NEG_FILL, 0.0).astype(np.float32))
    flops = units * 4 * BLOCK * slots * BLOCK * HEAD_DIM
    return pl.pallas_call(
        lambda *refs: sparse_attention_kernel(slots, blocks_here, *refs),
        out_shape=jax.ShapeDtypeStruct(queries.shape, queries.dtype),
        in_specs=[
            pl.BlockSpec(memory_space=pltpu.VMEM),
            pl.BlockSpec(memory_space=pltpu.VMEM),
            pl.BlockSpec(memory_space=pltpu.SMEM),
            pl.BlockSpec(memory_space=pltpu.VMEM),
            pl.BlockSpec(memory_space=pltpu.VMEM),
        ],
        out_specs=pl.BlockSpec(memory_space=pltpu.VMEM),
        scratch_shapes=[
            pltpu.VMEM((slots * BLOCK, HEAD_DIM), jnp.bfloat16),
            pltpu.VMEM((slots * BLOCK, HEAD_DIM), jnp.bfloat16),
        ],
        cost_estimate=pl.CostEstimate(
            flops=flops,
            transcendentals=units * BLOCK * slots * BLOCK,
            bytes_accessed=2 * queries.size * 2 + kv_all.size * 2,
        ),
    )(queries, kv_all, index, col_bias, causal_bias)


SCAN_SHIFTS = (2, 4, 8, 16)


def carry_scan_kernel(s_ref, a_ref, o_ref, cur_s, cur_a, got_s, got_a, sems):
    n = lax.axis_size("ctx")
    me = lax.axis_index("ctx")
    tp = lax.axis_index("tp")
    shifts = (1,) + SCAN_SHIFTS
    barrier = pltpu.get_barrier_semaphore()
    partners = sorted({k % n for k in shifts} | {(-k) % n for k in shifts})
    for k in partners:
        pl.semaphore_signal(
            barrier, inc=1, device_id=(lax.rem(me + k, n), tp), device_id_type=pl.DeviceIdType.MESH
        )
    pl.semaphore_wait(barrier, len(partners))

    def send(slot, k, src_s, src_a):
        target = (lax.rem(me + k, n), tp)
        copies = [
            pltpu.make_async_remote_copy(
                src_ref=src,
                dst_ref=dst.at[slot],
                send_sem=sems.at[part, 0, slot],
                recv_sem=sems.at[part, 1, slot],
                device_id=target,
                device_id_type=pl.DeviceIdType.MESH,
            )
            for part, (src, dst) in enumerate(((src_s, got_s), (src_a, got_a)))
        ]
        for copy in copies:
            copy.start()
        return copies

    def keep_of(k):
        return ((me - k + n) // n).astype(jnp.float32)

    first = send(0, 1, s_ref, a_ref) + send(1, 2, s_ref, a_ref)
    for copy in first:
        copy.wait()
    keep1, keep2 = keep_of(1), keep_of(2)
    a1, a2 = got_a[0], got_a[1]
    state = keep1 * (got_s[0] + a1 * (keep2 * got_s[1]))
    decay = (keep1 * a1 + (1.0 - keep1)) * (keep2 * a2 + (1.0 - keep2))
    for j, k in enumerate(SCAN_SHIFTS):
        cur_s[j] = state
        cur_a[j] = decay
        slot = j + 2
        for copy in send(slot, k, cur_s.at[j], cur_a.at[j]):
            copy.wait()
        keep = keep_of(k)
        state = cur_s[j] + cur_a[j] * (keep * got_s[slot])
        decay = cur_a[j] * (keep * got_a[slot] + (1.0 - keep))
    o_ref[...] = state


def carry_scan(local_state, carry_decay):
    rounds = len(SCAN_SHIFTS)
    slots = rounds + 2
    return pl.pallas_call(
        carry_scan_kernel,
        out_shape=jax.ShapeDtypeStruct(local_state.shape, local_state.dtype),
        in_specs=[pl.BlockSpec(memory_space=pltpu.VMEM)] * 2,
        out_specs=pl.BlockSpec(memory_space=pltpu.VMEM),
        scratch_shapes=[
            pltpu.VMEM((rounds,) + local_state.shape, jnp.float32),
            pltpu.VMEM((rounds,) + carry_decay.shape, jnp.float32),
            pltpu.VMEM((slots,) + local_state.shape, jnp.float32),
            pltpu.VMEM((slots,) + carry_decay.shape, jnp.float32),
            pltpu.SemaphoreType.DMA((2, 2, slots)),
        ],
        compiler_params=pltpu.CompilerParams(collective_id=0, has_side_effects=True),
    )(local_state, carry_decay)


def tp_sum_kernel(x_ref, o_ref, got, sems):
    n = lax.axis_size("tp")
    me = lax.axis_index("tp")
    row = lax.axis_index("ctx")
    barrier = pltpu.get_barrier_semaphore()
    for k in range(1, n):
        pl.semaphore_signal(
            barrier, inc=1, device_id=(row, lax.rem(me + k, n)), device_id_type=pl.DeviceIdType.MESH
        )
    pl.semaphore_wait(barrier, n - 1)
    copies = []
    for k in range(1, n):
        copy = pltpu.make_async_remote_copy(
            src_ref=x_ref,
            dst_ref=got.at[me],
            send_sem=sems.at[0, k],
            recv_sem=sems.at[1, k],
            device_id=(row, lax.rem(me + k, n)),
            device_id_type=pl.DeviceIdType.MESH,
        )
        copy.start()
        copies.append(copy)
    got[me] = x_ref[...]
    for k in range(1, n):
        copies[k - 1].wait_send()
        arriving = pltpu.make_async_remote_copy(
            src_ref=x_ref,
            dst_ref=got.at[lax.rem(me - k + n, n)],
            send_sem=sems.at[0, k],
            recv_sem=sems.at[1, k],
            device_id=(row, lax.rem(me + k, n)),
            device_id_type=pl.DeviceIdType.MESH,
        )
        arriving.wait_recv()
    total = got[0]
    for j in range(1, n):
        total = total + got[j]
    o_ref[...] = total


def tp_sum(values):
    n = lax.axis_size("tp")
    rows = values.size // 128
    shaped = jnp.pad(values.reshape(rows, 128), ((0, (-rows) % 8), (0, 0)))
    out = pl.pallas_call(
        tp_sum_kernel,
        out_shape=jax.ShapeDtypeStruct(shaped.shape, shaped.dtype),
        in_specs=[pl.BlockSpec(memory_space=pltpu.VMEM)],
        out_specs=pl.BlockSpec(memory_space=pltpu.VMEM),
        scratch_shapes=[
            pltpu.VMEM((n,) + shaped.shape, shaped.dtype),
            pltpu.SemaphoreType.DMA((2, n)),
        ],
        compiler_params=pltpu.CompilerParams(collective_id=1, has_side_effects=True),
    )(shaped)
    return out.reshape(-1)[: values.size]


def mamba_mix(ssm_input, gate, state_in, state_out, step_size, decay_log, skip_gain, norm_gain):
    careful = lax.Precision.HIGH
    row_count = ssm_input.shape[0]
    head_count = step_size.shape[1]
    inner_width = ssm_input.shape[1]
    inputs = ssm_input.astype(jnp.float32).reshape(row_count, head_count, SSM_HEAD_DIM)
    in_map = state_in.astype(jnp.float32)
    out_map = state_out.astype(jnp.float32)
    log_steps = -jnp.exp(decay_log)[None, :] * step_size
    cumulative = jnp.cumsum(log_steps, axis=0)
    grouped_per_head = cumulative.T
    lower = jnp.arange(row_count)[:, None] >= jnp.arange(row_count)[None, :]
    decay = jnp.where(
        lower[None],
        jnp.exp(jnp.minimum(grouped_per_head[:, :, None] - grouped_per_head[:, None, :], 0.0)),
        0.0,
    )
    inner = jnp.dot(state_out, state_in.T, preferred_element_type=jnp.float32)
    weighted = inputs * step_size[:, :, None]
    within = jnp.einsum("hts,shp->thp", decay * inner[None], weighted, precision=careful)
    tail = jnp.exp(cumulative[-1][None, :] - cumulative)
    local_state = jnp.einsum(
        "sn,shp->nhp", in_map, weighted * tail[:, :, None], precision=careful
    ).reshape(D_STATE, inner_width)
    carry_decay = jnp.repeat(jnp.exp(cumulative[-1]), SSM_HEAD_DIM)[None, :]

    incoming = carry_scan(local_state, carry_decay)

    from_past = jnp.dot(
        out_map, incoming, precision=careful, preferred_element_type=jnp.float32
    ).reshape(row_count, head_count, SSM_HEAD_DIM)
    from_past = from_past * jnp.exp(cumulative)[:, :, None]
    mixed = (within + from_past + skip_gain[None, :, None] * inputs).reshape(row_count, inner_width)
    gate_full = gate.astype(jnp.float32)
    gated = mixed * gate_full * jax.nn.sigmoid(gate_full)
    squares = tp_sum(jnp.sum(gated * gated, axis=1))
    scaled = gated * lax.rsqrt(squares / INNER + 1e-05)[:, None] * norm_gain[None, :]
    return scaled.astype(jnp.bfloat16)


def local(
    queries,
    keys,
    values,
    vertical,
    slash,
    block_position,
    ssm_input,
    gate,
    state_in,
    state_out,
    step_size,
    decay_log,
    skip_gain,
    norm_gain,
):
    kv_local = jnp.stack((keys, values))
    kv_local, ssm_input, step_size, decay_log, state_in = lax.optimization_barrier(
        (kv_local, ssm_input, step_size, decay_log, state_in)
    )
    attention_out = attend_sparse(queries, kv_local, vertical, slash, block_position)
    recurrent_mixer_result = mamba_mix(
        ssm_input, gate, state_in, state_out, step_size, decay_log, skip_gain, norm_gain
    )
    return (attention_out, recurrent_mixer_result)


def solution(mesh):
    return jax.shard_map(
        local,
        mesh=mesh,
        in_specs=(
            P("ctx", "tp"),
            P("ctx", "tp"),
            P("ctx", "tp"),
            P("tp", None),
            P("tp", None),
            P(),
            P("ctx", "tp"),
            P("ctx", "tp"),
            P("ctx", None),
            P("ctx", None),
            P("ctx", "tp"),
            P("tp"),
            P("tp"),
            P("tp"),
        ),
        out_specs=(P("ctx", "tp"), P("ctx", "tp")),
        check_vma=False,
    )
```
